768 devices in a mesh: seq: 12 (over z_hi, x), head: 64 (over z_lo, y, core).
Axes of the slice: x: 4, y: 8, z: 12 (z_hi: 3, z_lo: 4; z = z_hi * 4 + z_lo), core: 2. Of those that a mesh axis runs over, the one named last changes fastest.
Arguments:
- out_grad: bfloat16 [6144, 8192], P('seq'), may hold values from -6 to 6
- out_weight: bfloat16 [8192, 8192], P(None, 'head'), may hold values from -0.0625 to 0.0625
- gate_input: bfloat16 [6144, 8192], P('seq', 'head'), may hold values from -6 to 6
- scan_output: bfloat16 [6144, 8192], P('seq', 'head'), may hold values from -6 to 6
- step_size: float32 [6144, 128], P('seq', 'head'), may hold values from 0.5 to 2
- log_decay: float32 [6144, 128], P('seq', 'head'), may hold values from -1 to 0
- input_map: bfloat16 [6144, 4, 256], P('seq'), may hold values from -0.375 to 0.375
- output_map: bfloat16 [6144, 4, 256], P('seq'), may hold values from -0.375 to 0.375
- skip_gain: float32 [128], P('head'), may hold values from 0.5 to 1.5
Outputs:
- input_grad: bfloat16 [6144, 8192], P('seq', 'head')
- gate_grad: bfloat16 [6144, 8192], P('seq', 'head')
- weight_grad: bfloat16 [8192, 8192], P(None, 'head')
The draws below stay inside these ranges and needn't reach their ends.
All inputs are finite; a program needn't handle non-finite values.
Results may differ from the reference program's by a relative error of at most 0.02.
Values may be sent and summed in bfloat16 or wider, within the bound.
No kernel may reach another device: no remote copies, remote signals or barrier semaphores. Data moves between devices by JAX's collectives and lax.ppermute only.
A program may use at most 64 MiB of HBM per device.

```python
import math
from functools import partial
import jax
import jax.numpy as jnp
from jax import lax

D = 8192
HEAD_COUNT = 128
P_SIZE = 64
N = 256
G = 4
L_DEV = 512
TOKEN_COUNT = 6144
N_SEQ = 12


def draw_log_decay(key, part):
    random_subkeys = jax.random.split(key, 6)
    fast_share = 0.5
    fast_head = jax.random.uniform(random_subkeys[0], (HEAD_COUNT,)) < fast_share
    fast_rate = jax.random.uniform(random_subkeys[1], (HEAD_COUNT,), minval=0.06, maxval=0.1)
    slow_rate = jnp.exp(jax.random.uniform(random_subkeys[2], (HEAD_COUNT,), minval=math.log(0.1), maxval=math.log(0.8))) / TOKEN_COUNT
    decay_speed = jnp.where(fast_head, fast_rate, slow_rate)
    jaggedness = jax.random.uniform(random_subkeys[3], (TOKEN_COUNT, HEAD_COUNT), minval=0.5, maxval=1.5)
    spike_positions = jax.random.randint(random_subkeys[4], (3,), 0, TOKEN_COUNT)
    spike_selected = jnp.any(jnp.arange(TOKEN_COUNT)[:, None] == spike_positions[None, :], axis=1)
    spike_magnitude = jax.random.uniform(random_subkeys[5], (TOKEN_COUNT, HEAD_COUNT), minval=0.22, maxval=0.5)
    logarithm_values = -decay_speed[None, :] * jaggedness - jnp.where(spike_selected[:, None], spike_magnitude, 0.0)
    return logarithm_values.astype(jnp.float32)


def block_levels(own_key, extent, cuts, smallest, largest):
    def one(axis_at, parts):
        heights = jax.random.uniform(jax.random.fold_in(jax.random.fold_in(own_key, 6), axis_at), (parts,), jnp.float32, smallest / len(cuts), largest / len(cuts))
        return jnp.repeat(jnp.exp(heights), extent[axis_at] // parts).reshape((-1,) + (1,) * (len(extent) - axis_at - 1))

    factor_of = one(*cuts[0])
    for cut in cuts[1:]:
        factor_of = factor_of * one(*cut)
    return factor_of


def centred(stream_key, dims, deviation, bound, cuts=(), held_as=jnp.bfloat16):
    values = deviation * jax.random.normal(stream_key, dims, jnp.float32)
    if cuts:
        values = values * block_levels(stream_key, dims, cuts, -0.22, 0.18)
    return jnp.clip(values, -bound, bound).astype(held_as)


def setup_inputs(seed: int = 0) -> dict:
    splits = jax.random.split(jax.random.key(seed), 10)
    out_grad = centred(splits[0], (TOKEN_COUNT, D), 1.0, 6.0, ((0, 12),))
    out_weight = centred(splits[1], (HEAD_COUNT * P_SIZE, D), (HEAD_COUNT * P_SIZE) ** -0.5, 0.0625, ((1, 64),))
    gate_input = centred(splits[2], (TOKEN_COUNT, HEAD_COUNT * P_SIZE), 1.0, 6.0, ((0, 12), (1, 64)))
    scan_output = centred(splits[3], (TOKEN_COUNT, HEAD_COUNT * P_SIZE), 1.0, 6.0, ((0, 12), (1, 64)))
    step_size = jnp.clip(0.5 + 1.5 * jax.random.uniform(splits[4], (TOKEN_COUNT, HEAD_COUNT), jnp.float32) ** block_levels(splits[4], (TOKEN_COUNT, HEAD_COUNT), ((0, 12), (1, 64)), -0.2, 0.2), 0.5, 2.0)
    log_decay = draw_log_decay(jax.random.fold_in(splits[9], 71), 0)
    input_map = centred(splits[6], (TOKEN_COUNT, G, N), N ** -0.5, 0.375, ((0, 12),))
    output_map = centred(splits[7], (TOKEN_COUNT, G, N), N ** -0.5, 0.375, ((0, 12),))
    skip_gain = jnp.clip(0.5 + 1.0 * jax.random.uniform(splits[8], (HEAD_COUNT,), jnp.float32) ** block_levels(splits[8], (HEAD_COUNT,), ((0, 64),), -0.2, 0.2), 0.5, 1.5)
    return {"out_grad": out_grad, "out_weight": out_weight, "gate_input": gate_input, "scan_output": scan_output, "step_size": step_size, "log_decay": log_decay, "input_map": input_map, "output_map": output_map, "skip_gain": skip_gain}


highest = lax.Precision.HIGHEST

def block_grads(skip_gain, carried, inputs):
    decay_block, grad_block, step_block, in_block, out_block = inputs
    heads_group = HEAD_COUNT // G
    cumulative = jnp.cumsum(decay_block, axis=0)
    block_total = cumulative[-1]
    intersection = jnp.einsum('tgn,sgn->gts', in_block.astype(jnp.float32), out_block.astype(jnp.float32), precision=highest)
    intersection = jnp.repeat(intersection, heads_group, axis=0)
    positions = jnp.arange(decay_block.shape[0])
    upper_mask = positions[:, None] <= positions[None, :]
    spread = cumulative.T[:, None, :] - cumulative.T[:, :, None]
    factor = jnp.where(upper_mask[None], jnp.exp(jnp.minimum(spread, 0.0)), 0.0)
    weights = (intersection * factor).astype(jnp.bfloat16)
    grad_float = grad_block.astype(jnp.float32)
    inside_term = jnp.einsum('hts,shp->thp', weights.astype(jnp.float32), grad_float, precision=highest)
    in_heads = jnp.repeat(in_block.astype(jnp.float32), heads_group, axis=1)
    out_heads = jnp.repeat(out_block.astype(jnp.float32), heads_group, axis=1)
    carried_term = jnp.einsum('hpn,thn->thp', carried, in_heads, precision=highest)
    tail_decay = jnp.exp(block_total[None, :] - cumulative)
    result = step_block[:, :, None] * (inside_term + tail_decay[:, :, None] * carried_term) + skip_gain[None, :, None] * grad_float
    weighted = grad_float * jnp.exp(cumulative)[:, :, None]
    local_term = jnp.einsum('thp,thn->hpn', weighted, out_heads, precision=highest)
    passed = local_term + jnp.exp(block_total)[:, None, None] * carried
    return (passed, result.astype(jnp.bfloat16))

def reference(out_grad, out_weight, gate_input, scan_output, step_size, log_decay, input_map, output_map, skip_gain):
    upstream = jnp.dot(out_grad, out_weight.T, preferred_element_type=jnp.float32)
    gate_value = gate_input.astype(jnp.float32)
    sigmoid_gate = jax.nn.sigmoid(gate_value)
    silu_gate = gate_value * sigmoid_gate
    saved_output = scan_output.astype(jnp.float32)
    gated_rows = (saved_output * silu_gate).astype(jnp.bfloat16)
    gate_grad = (upstream * saved_output * sigmoid_gate * (1.0 + gate_value * (1.0 - sigmoid_gate))).astype(jnp.bfloat16)
    scan_grad = (upstream * silu_gate).astype(jnp.bfloat16)
    grad_scale = 1.0 / math.sqrt(TOKEN_COUNT)

    def add_block(block_index, total):
        start = (block_index * L_DEV).astype(jnp.int32)
        rows_gated = lax.dynamic_slice_in_dim(gated_rows, start, L_DEV, 0)
        rows_grad = lax.dynamic_slice_in_dim(out_grad, start, L_DEV, 0)
        block_part = (jnp.dot(rows_gated.T, rows_grad, preferred_element_type=jnp.float32) * grad_scale).astype(jnp.bfloat16)
        return total + block_part.astype(jnp.float32)
    weight_grad = lax.fori_loop(0, N_SEQ, add_block, jnp.zeros((HEAD_COUNT * P_SIZE, D), jnp.float32)).astype(jnp.bfloat16)
    inputs = (log_decay.reshape(N_SEQ, L_DEV, HEAD_COUNT), scan_grad.reshape(N_SEQ, L_DEV, HEAD_COUNT, P_SIZE), step_size.reshape(N_SEQ, L_DEV, HEAD_COUNT), input_map.reshape(N_SEQ, L_DEV, G, N), output_map.reshape(N_SEQ, L_DEV, G, N))
    initial = jnp.zeros((HEAD_COUNT, P_SIZE, N), jnp.float32)
    final_state, results = lax.scan(partial(block_grads, skip_gain), initial, inputs, reverse=True)
    input_grad = results.reshape(TOKEN_COUNT, HEAD_COUNT * P_SIZE)
    return (input_grad, gate_grad, weight_grad)
```

```python
import math

import jax
import jax.numpy as jnp
from jax import lax
from jax.sharding import PartitionSpec as P

HEAD_COUNT = 128
G = 4
RING = 4


highest = lax.Precision.HIGHEST
f32 = jnp.float32
bf16 = jnp.bfloat16


def along_x(block, step):
    rows = lax.axis_size("seq")
    route = [(i, i // RING * RING + (i + step) % RING) for i in range(rows)]
    return lax.ppermute(block, "seq", route)


def along_z(block, step):
    size = lax.axis_size("seq")
    route = [(i, (i + RING * step) % size) for i in range(size)]
    return lax.ppermute(block, "seq", route)


def gather_x(mine):
    half = mine.shape[0] // 2
    a, b = mine[:half], mine[half:]
    prev_a = along_x(a, 1)
    next_b = along_x(b, -1)
    prev_b = along_x(b, 1)
    next_a = along_x(a, -1)
    opposite_a = along_x(prev_a, 1)
    opposite_b = along_x(next_b, -1)
    return [(a, b), (next_a, next_b), (opposite_a, opposite_b), (prev_a, prev_b)]


def place(quarters, x):
    half, rows, columns = quarters[0][0].shape
    out = jnp.zeros((2, half, RING, rows, columns), quarters[0][0].dtype)
    for j, pair in enumerate(quarters):
        for k, piece in enumerate(pair):
            out = lax.dynamic_update_slice(
                out, piece[None, :, None], (k, 0, (x + j) % RING, 0, 0)
            )
    return out.reshape(2 * half, RING, rows, columns)


def scatter_x(quarters):
    half = quarters[0].shape[0] // 2
    (own_a, own_b), (next_a, next_b), (far_a, far_b), (prev_a, prev_b) = [
        (q[:half], q[half:]) for q in quarters
    ]
    from_prev_a = along_x(far_a, 1)
    from_next_b = along_x(far_b, -1)
    got_b = along_x(next_b, 1)
    got_a = along_x(prev_a, -1)
    add = lambda *terms: sum(t.astype(f32) for t in terms)
    more_a = along_x(add(next_a, from_prev_a).astype(bf16), 1)
    more_b = along_x(add(prev_b, from_next_b).astype(bf16), -1)
    total_a = add(own_a, got_a, more_a).astype(bf16)
    total_b = add(own_b, got_b, more_b).astype(bf16)
    return jnp.concatenate([total_a, total_b], axis=0)


def on_device(
    out_grad,
    out_weight,
    gate_input,
    scan_output,
    step_size,
    log_decay,
    input_map,
    output_map,
    skip_gain,
):
    length, width = out_grad.shape
    heads_here = log_decay.shape[1]
    columns_here = gate_input.shape[1]
    head_width = columns_here // heads_here
    seq_size = lax.axis_size("seq")
    head_size = lax.axis_size("head")
    rows_z = seq_size // RING
    quarter = columns_here // RING
    me = lax.axis_index("seq")
    x = me % RING
    z = me // RING

    weight_quarter = lax.dynamic_index_in_dim(
        out_weight.reshape(head_size, RING, quarter, out_weight.shape[1]), x, 1, keepdims=False
    )
    rows_quarter = lax.all_to_all(weight_quarter, "head", split_axis=0, concat_axis=0, tiled=True)
    row_panel = place(gather_x(rows_quarter), x).reshape(
        head_size, columns_here, out_weight.shape[1]
    )

    gate_value = gate_input.astype(f32)
    sigmoid_gate = jax.nn.sigmoid(gate_value)
    silu_gate = gate_value * sigmoid_gate
    saved_output = scan_output.astype(f32)
    gated_rows = (saved_output * silu_gate).astype(bf16)

    grad_scale = 1.0 / math.sqrt(length * seq_size)
    gated_turned = jnp.take(
        gated_rows.T.reshape(RING, quarter, length), (x + jnp.arange(RING)) % RING, axis=0
    ).reshape(columns_here, length)
    block_part = (
        jnp.einsum(
            "kt,tbd->bkd",
            gated_turned,
            out_grad.reshape(length, head_size, width // head_size),
            preferred_element_type=f32,
        )
        * grad_scale
    ).astype(bf16)
    parts = block_part.reshape(head_size, RING, quarter, width // head_size)
    quarter_sum = scatter_x([parts[:, j] for j in range(RING)])
    pieces = lax.all_to_all(quarter_sum, "head", split_axis=0, concat_axis=0, tiled=True)
    window = -(-head_size // rows_z)
    starts = [k * (head_size - window) // (rows_z - 1) for k in range(rows_z)]
    start_of = jnp.array(starts, jnp.int32)

    def window_of(k):
        return lax.dynamic_slice_in_dim(pieces, start_of[k % rows_z], window, 0)

    above = along_z(window_of(z + 1), 1)
    below = along_z(window_of(z + 2), 2)
    reduced = (window_of(z).astype(f32) + above.astype(f32) + below.astype(f32)).astype(bf16)
    got_lower = along_z(reduced, 1)
    got_upper = along_z(reduced, 2)
    summed = pieces
    for offset, piece in ((0, reduced), (2, got_lower), (1, got_upper)):
        summed = lax.dynamic_update_slice_in_dim(
            summed, piece, start_of[(z + offset) % rows_z], 0
        )
    weight_grad = place(gather_x(summed), x).reshape(
        head_size * columns_here, width // head_size
    )

    group_index = lax.axis_index("head") * heads_here // (HEAD_COUNT // G)
    in_group = lax.dynamic_index_in_dim(input_map, group_index, 1, keepdims=False)
    out_group = lax.dynamic_index_in_dim(output_map, group_index, 1, keepdims=False)
    cumulative = jnp.cumsum(log_decay, axis=0)
    block_total = cumulative[-1]
    totals = lax.all_to_all(
        jnp.broadcast_to(block_total, (seq_size, heads_here)),
        "seq",
        split_axis=0,
        concat_axis=0,
        tiled=True,
    )
    upstream = jnp.einsum(
        "tbd,bkd->tk",
        out_grad.reshape(length, head_size, width // head_size),
        row_panel,
        preferred_element_type=f32,
    )
    gate_grad = (
        upstream * saved_output * sigmoid_gate * (1.0 + gate_value * (1.0 - sigmoid_gate))
    ).astype(bf16)
    scan_grad = (upstream * silu_gate).astype(bf16)
    grad_heads = scan_grad.reshape(length, heads_here, head_width)
    grad_float = grad_heads.astype(f32)
    weighted = grad_float * jnp.exp(cumulative)[:, :, None]
    local_term = jnp.einsum(
        "thp,tn->hpn", weighted, out_group.astype(f32), precision=highest
    )

    sent = local_term.astype(bf16)
    others = [along_x(sent, -j) for j in range(1, RING)]
    positions_x = jnp.arange(RING)
    row_totals = lax.dynamic_slice_in_dim(totals, z * RING, RING, 0)

    def decay_between(first, last):
        inside = (positions_x >= first) & (positions_x < last)
        return jnp.exp(jnp.sum(jnp.where(inside[:, None], row_totals, 0.0), axis=0))[:, None, None]

    in_row = jnp.zeros_like(local_term)
    row_sum = decay_between(0, x) * local_term
    for j, term in enumerate(others, 1):
        place_x = (x + j) % RING
        term = term.astype(f32)
        in_row += jnp.where(x + j < RING, decay_between(x + 1, place_x), 0.0) * term
        row_sum += decay_between(0, place_x) * term
    sent_row = row_sum.astype(bf16)
    sum_by_row = jnp.sum(totals.reshape(rows_z, RING, heads_here), axis=1)
    from_rows = jnp.zeros_like(local_term)
    positions_z = jnp.arange(rows_z)
    for j in range(1, rows_z):
        term = along_z(sent_row, -j).astype(f32)
        inside = (positions_z > z) & (positions_z < z + j)
        decay = jnp.exp(jnp.sum(jnp.where(inside[:, None], sum_by_row, 0.0), axis=0))
        from_rows += jnp.where(z + j < rows_z, decay, 0.0)[:, None, None] * term
    carried = in_row + decay_between(x + 1, RING) * from_rows

    intersection = jnp.dot(in_group, out_group.T, preferred_element_type=f32)
    positions = jnp.arange(length)
    upper_mask = positions[:, None] <= positions[None, :]
    spread = cumulative.T[:, None, :] - cumulative.T[:, :, None]
    factor = jnp.where(upper_mask[None], jnp.exp(jnp.minimum(spread, 0.0)), 0.0)
    weights = (intersection[None] * factor).astype(bf16)
    inside_term = jnp.einsum(
        "hts,shp->thp", weights, grad_heads, preferred_element_type=f32
    )
    carried_term = jnp.einsum(
        "hpn,tn->thp", carried, in_group.astype(f32), precision=highest
    )
    tail_decay = jnp.exp(block_total[None, :] - cumulative)
    result = (
        step_size[:, :, None] * (inside_term + tail_decay[:, :, None] * carried_term)
        + skip_gain[None, :, None] * grad_float
    )
    input_grad = result.astype(bf16).reshape(length, columns_here)
    return (input_grad, gate_grad, weight_grad)


def solution(mesh):
    in_specs = (
        P("seq", None),
        P(None, "head"),
        P("seq", "head"),
        P("seq", "head"),
        P("seq", "head"),
        P("seq", "head"),
        P("seq", None, None),
        P("seq", None, None),
        P("head"),
    )
    out_specs = (P("seq", "head"), P("seq", "head"), P(None, "head"))
    return jax.shard_map(
        on_device, mesh=mesh, in_specs=in_specs, out_specs=out_specs, check_vma=False
    )
```

```python
import functools
import math

import jax
import jax.numpy as jnp
from jax import lax
from jax.experimental import pallas as pl
from jax.experimental.pallas import tpu as pltpu
from jax.sharding import PartitionSpec as P

HEAD_COUNT = 128
G = 4
RING = 4
EXTRA = 16

f32 = jnp.float32
bf16 = jnp.bfloat16
VMEM = pl.BlockSpec(memory_space=pltpu.VMEM)
SMEM = pl.BlockSpec(memory_space=pltpu.SMEM)
NT = (((1,), (1,)), ((), ()))
TN = (((0,), (0,)), ((), ()))


def by_head(columns, width):
    rows, heads = columns.shape
    head = lax.broadcasted_iota(jnp.int32, (rows, heads * width), 1) // width
    out = jnp.broadcast_to(columns[:, :1], (rows, heads * width))
    for h in range(1, heads):
        out = jnp.where(head == h, columns[:, h : h + 1], out)
    return out


def part_kernel(scale, gate, saved, grad, out, turned):
    @pl.when(pl.program_id(0) == 0)
    def _():
        value = gate[...].astype(f32)
        gated = saved[...].astype(f32) * (value * jax.nn.sigmoid(value))
        turned[...] = gated.astype(bf16).astype(f32).T.astype(bf16)

    product = jnp.dot(turned[...], grad[...], preferred_element_type=f32) * scale
    quarters, blocks, rows, columns = out.shape
    for b in range(blocks):
        piece = product[:, b * columns : (b + 1) * columns].astype(bf16)
        out[:, b] = piece.reshape(quarters, rows, columns)


def write_log(message, h, total):
    rows = message.shape[2] - EXTRA
    high = total.astype(bf16).astype(f32)
    middle = (total - high).astype(bf16).astype(f32)
    low = total - high - middle
    place = lax.broadcasted_iota(jnp.int32, (EXTRA, total.shape[1]), 0)
    tail = jnp.where(
        place == 0, high, jnp.where(place == 1, middle, jnp.where(place == 2, low, 0.0))
    )
    for k in range(message.shape[0]):
        message[k, h, rows:] = tail.astype(bf16)


def read_log(message, k, h):
    rows = message.shape[2] - EXTRA
    tail = message[k, h, rows:].astype(f32)
    return tail[0:1] + tail[1:2] + tail[2:3]


def upstream_kernel(
    grad, panel, gate, saved, cumulative, out_group, gate_grad, scan_grad, message, total
):
    step = pl.program_id(0)
    quarters, blocks, rows, columns = panel.shape
    weights = jnp.concatenate(
        [panel[:, b].reshape(quarters * rows, columns) for b in range(blocks)], axis=1
    )
    product = lax.dot_general(grad[...], weights, NT, preferred_element_type=f32)

    @pl.when(step == 0)
    def _():
        total[...] = product

    @pl.when(step > 0)
    def _():
        total[...] += product

    @pl.when(step == pl.num_programs(0) - 1)
    def _():
        upstream = total[...]
        value = gate[...].astype(f32)
        sig = jax.nn.sigmoid(value)
        gate_grad[...] = (
            upstream * saved[...].astype(f32) * sig * (1.0 + value * (1.0 - sig))
        ).astype(bf16)
        scan = (upstream * (value * sig)).astype(bf16)
        scan_grad[...] = scan
        heads = cumulative.shape[1]
        width = scan.shape[1] // heads
        weighted = scan.astype(f32) * by_head(jnp.exp(cumulative[...]), width)
        local = lax.dot_general(
            weighted.astype(bf16), out_group[...], TN, preferred_element_type=f32
        )
        states = local.shape[1]
        for h in range(heads):
            term = local[h * width : (h + 1) * width].astype(bf16)
            for k in range(message.shape[0]):
                message[k, h, :width] = term
            last = jnp.broadcast_to(cumulative[cumulative.shape[0] - 1 :, h : h + 1], (1, states))
            write_log(message, h, last)


def row_kernel(x_ref, received, message, in_row, tail_log):
    x = x_ref[0]
    ring, heads, rows, states = received.shape
    width = rows - EXTRA
    for h in range(heads):
        carry = jnp.zeros((width, states), f32)
        inside = carry
        logs = jnp.zeros((1, states), f32)
        tail = logs
        for j in reversed(range(ring)):
            log = read_log(received, j, h)
            inside = jnp.where(x == j, carry, inside)
            tail = jnp.where(x == j, logs, tail)
            carry = received[j, h, :width].astype(f32) + jnp.exp(log) * carry
            logs = logs + log
        in_row[h] = inside
        tail_log[h] = jnp.broadcast_to(tail, tail_log.shape[1:])
        for k in range(message.shape[0]):
            message[k, h, :width] = carry.astype(bf16)
        write_log(message, h, logs)


def inside_kernel(in_group, out_group, cumulative, turned, scan_grad, step_size, skip_gain, out):
    length, heads = cumulative.shape
    width = scan_grad.shape[1] // heads
    size = 128
    for start in range(0, length, size):
        here = slice(start, start + size)
        dots = lax.dot_general(
            in_group[here], out_group[start:], NT, preferred_element_type=f32
        )
        t = lax.broadcasted_iota(jnp.int32, dots.shape, 0)
        s = lax.broadcasted_iota(jnp.int32, dots.shape, 1)
        terms = []
        for h in range(heads):
            spread = turned[h : h + 1, start:] - cumulative[here, h : h + 1]
            factor = jnp.where(t <= s, jnp.exp(jnp.minimum(spread, 0.0)), 0.0)
            terms.append(
                jnp.dot(
                    (dots * factor).astype(bf16),
                    scan_grad[start:, h * width : (h + 1) * width],
                    preferred_element_type=f32,
                )
            )
        inside = jnp.concatenate(terms, axis=1)
        out[here] = by_head(step_size[here], width) * inside + by_head(
            jnp.broadcast_to(skip_gain[...], (size, heads)), width
        ) * scan_grad[here].astype(f32)


def carried_kernel(
    z_ref, received, in_row, tail_log, in_group, cumulative, step_size, partial, out
):
    z = z_ref[0]
    rows_z, heads, rows, states = received.shape
    width = rows - EXTRA
    length = cumulative.shape[0]
    terms = []
    for h in range(heads):
        carry = jnp.zeros((width, states), f32)
        for j in reversed(range(1, rows_z)):
            term = received[j, h, :width].astype(f32)
            carry = jnp.where(j > z, term + jnp.exp(read_log(received, j, h)) * carry, carry)
        carried = in_row[h] + jnp.exp(tail_log[h, 0:1]) * carry
        terms.append(
            lax.dot_general(in_group[...], carried.astype(bf16), NT, preferred_element_type=f32)
        )
    decay = jnp.exp(cumulative[length - 1 :] - cumulative[...])
    scale = by_head(step_size[...] * decay, width)
    out[...] = (partial[...] + scale * jnp.concatenate(terms, axis=1)).astype(bf16)


def cost(flops, bytes_accessed, transcendentals=0):
    return pl.CostEstimate(
        flops=flops, bytes_accessed=bytes_accessed, transcendentals=transcendentals
    )


def to_group(blocks, groups):
    return lax.all_to_all(
        blocks, "seq", split_axis=0, concat_axis=0, tiled=True, axis_index_groups=groups
    )


def after(value, *others):
    return lax.optimization_barrier((value, *others))[0]


def on_device(
    out_grad,
    out_weight,
    gate_input,
    scan_output,
    step_size,
    log_decay,
    input_map,
    output_map,
    skip_gain,
):
    length, width = out_grad.shape
    heads_here = log_decay.shape[1]
    columns_here = gate_input.shape[1]
    head_width = columns_here // heads_here
    seq_size = lax.axis_size("seq")
    head_size = lax.axis_size("head")
    rows_z = seq_size // RING
    quarter = columns_here // RING
    column_block = width // head_size
    states = input_map.shape[2]
    message_rows = head_width + EXTRA
    me = lax.axis_index("seq")
    x = (me % RING).astype(jnp.int32)
    z = (me // RING).astype(jnp.int32)
    rings = [[r * RING + i for i in range(RING)] for r in range(rows_z)]
    lines = [[r * RING + i for r in range(rows_z)] for i in range(RING)]
    steps = max(head_size // 4, 1)
    blocks = head_size // steps
    wide = blocks * column_block

    parts = pl.pallas_call(
        functools.partial(part_kernel, 1.0 / math.sqrt(length * seq_size)),
        name="block_parts",
        grid=(steps,),
        in_specs=[
            pl.BlockSpec((length, columns_here), lambda i: (0, 0)),
            pl.BlockSpec((length, columns_here), lambda i: (0, 0)),
            pl.BlockSpec((length, wide), lambda i: (0, i)),
        ],
        out_specs=pl.BlockSpec((RING, blocks, quarter, column_block), lambda i: (0, i, 0, 0)),
        out_shape=jax.ShapeDtypeStruct((RING, head_size, quarter, column_block), bf16),
        scratch_shapes=[pltpu.VMEM((columns_here, length), bf16)],
        cost_estimate=cost(2 * length * width * columns_here, 2 * length * width),
    )(gate_input, scan_output, out_grad)
    from_ring = to_group(parts, rings)
    quarter_sum = jnp.sum(from_ring.astype(f32), axis=0).astype(bf16)

    weight_quarter = lax.dynamic_index_in_dim(
        after(out_weight, parts).reshape(head_size, RING, quarter, column_block),
        x,
        1,
        keepdims=False,
    )
    rows_quarter = lax.all_to_all(weight_quarter, "head", split_axis=0, concat_axis=0, tiled=True)
    rows_quarter = after(rows_quarter, quarter_sum)
    panel = to_group(
        jnp.broadcast_to(rows_quarter[None], (RING, *rows_quarter.shape)), rings
    )

    pieces = lax.all_to_all(quarter_sum, "head", split_axis=0, concat_axis=0, tiled=True)
    window = -(-head_size // rows_z)
    starts = [k * (head_size - window) // (rows_z - 1) for k in range(rows_z)]
    from_line = to_group(jnp.stack([pieces[s : s + window] for s in starts]), lines)
    reduced = jnp.sum(from_line.astype(f32), axis=0).astype(bf16)
    all_windows = to_group(jnp.broadcast_to(reduced[None], (rows_z, *reduced.shape)), lines)
    ends = starts[1:] + [head_size]
    summed = jnp.concatenate(
        [all_windows[k, : ends[k] - starts[k]] for k in range(rows_z)], axis=0
    )
    all_quarters = to_group(jnp.broadcast_to(summed[None], (RING, *summed.shape)), rings)
    weight_grad = jnp.transpose(all_quarters, (1, 0, 2, 3)).reshape(
        head_size * columns_here, column_block
    )

    group_index = lax.axis_index("head") * heads_here // (HEAD_COUNT // G)
    in_group = lax.dynamic_index_in_dim(input_map, group_index, 1, keepdims=False)
    out_group = lax.dynamic_index_in_dim(output_map, group_index, 1, keepdims=False)
    cumulative = jnp.cumsum(log_decay, axis=0)
    whole = lambda shape: pl.BlockSpec(shape, lambda i: (0,) * len(shape))
    panel_shape = (length, columns_here)
    gate_grad, scan_grad, message = pl.pallas_call(
        upstream_kernel,
        name="upstream",
        grid=(steps,),
        in_specs=[
            pl.BlockSpec((length, wide), lambda i: (0, i)),
            pl.BlockSpec((RING, blocks, quarter, column_block), lambda i: (0, i, 0, 0)),
            whole(panel_shape),
            whole(panel_shape),
            whole((length, heads_here)),
            whole((length, states)),
        ],
        out_specs=[
            whole(panel_shape),
            whole(panel_shape),
            whole((RING, heads_here, message_rows, states)),
        ],
        out_shape=[
            jax.ShapeDtypeStruct(panel_shape, bf16),
            jax.ShapeDtypeStruct(panel_shape, bf16),
            jax.ShapeDtypeStruct((RING, heads_here, message_rows, states), bf16),
        ],
        scratch_shapes=[pltpu.VMEM(panel_shape, f32)],
        cost_estimate=cost(2 * length * width * columns_here, 2 * length * width),
    )(out_grad, panel, gate_input, scan_output, cumulative, out_group)

    state = (heads_here, head_width, states)
    by_place = to_group(message, rings)
    row_message, in_row, tail_log = pl.pallas_call(
        row_kernel,
        name="row_scan",
        in_specs=[SMEM, VMEM],
        out_specs=[VMEM, VMEM, VMEM],
        out_shape=[
            jax.ShapeDtypeStruct((rows_z, heads_here, message_rows, states), bf16),
            jax.ShapeDtypeStruct(state, f32),
            jax.ShapeDtypeStruct((heads_here, 8, states), f32),
        ],
        cost_estimate=cost(10**6, 10**6),
    )(x.reshape(1), by_place)
    by_row = to_group(row_message, lines)
    partial = pl.pallas_call(
        inside_kernel,
        name="inside",
        in_specs=[VMEM] * 7,
        out_specs=VMEM,
        out_shape=jax.ShapeDtypeStruct(panel_shape, f32),
        cost_estimate=cost(4 * 10**8, 2 * 10**6, 2 * length * length),
    )(
        in_group,
        out_group,
        cumulative,
        cumulative.T,
        scan_grad,
        step_size,
        skip_gain.reshape(1, heads_here),
    )
    input_grad = pl.pallas_call(
        carried_kernel,
        name="carried",
        in_specs=[SMEM] + [VMEM] * 7,
        out_specs=VMEM,
        out_shape=jax.ShapeDtypeStruct(panel_shape, bf16),
        cost_estimate=cost(10**8, 10**6),
    )(z.reshape(1), by_row, in_row, tail_log, in_group, cumulative, step_size, partial)
    return (input_grad, gate_grad, weight_grad)


def solution(mesh):
    in_specs = (
        P("seq", None),
        P(None, "head"),
        P("seq", "head"),
        P("seq", "head"),
        P("seq", "head"),
        P("seq", "head"),
        P("seq", None, None),
        P("seq", None, None),
        P("head"),
    )
    out_specs = (P("seq", "head"), P("seq", "head"), P(None, "head"))
    return jax.shard_map(
        on_device, mesh=mesh, in_specs=in_specs, out_specs=out_specs, check_vma=False
    )
```

```python
import functools
import math

import jax
import jax.numpy as jnp
from jax import lax
from jax.experimental import pallas as pl
from jax.experimental.pallas import tpu as pltpu
from jax.sharding import PartitionSpec as P

HEAD_COUNT = 128
G = 4
RING = 4
EXTRA = 16
PART_STEPS = 2

f32 = jnp.float32
bf16 = jnp.bfloat16
VMEM = pl.BlockSpec(memory_space=pltpu.VMEM)
SMEM = pl.BlockSpec(memory_space=pltpu.SMEM)
NT = (((1,), (1,)), ((), ()))
TN = (((0,), (0,)), ((), ()))


def by_head(columns, width):
    rows, heads = columns.shape
    head = lax.broadcasted_iota(jnp.int32, (rows, heads * width), 1) // width
    out = jnp.broadcast_to(columns[:, :1], (rows, heads * width))
    for h in range(1, heads):
        out = jnp.where(head == h, columns[:, h : h + 1], out)
    return out


def part_kernel(scale, x_ref, gate, saved, grad, *rest):
    outs, turned, ordered = rest[:RING], rest[RING], rest[RING + 1]
    blocks, rows, columns = outs[0].shape

    @pl.when(pl.program_id(0) == 0)
    def _():
        value = gate[...].astype(f32)
        gated = saved[...].astype(f32) * (value * jax.nn.sigmoid(value))
        turned[...] = gated.T
        for j in range(RING):
            start = pl.multiple_of((x_ref[0] + j) % RING * rows, rows)
            ordered[j * rows : (j + 1) * rows] = turned[pl.ds(start, rows)].astype(bf16)

    product = jnp.dot(ordered[...], grad[...], preferred_element_type=f32) * scale
    for b in range(blocks):
        piece = product[:, b * columns : (b + 1) * columns].astype(bf16)
        for j in range(RING):
            outs[j][b] = piece[j * rows : (j + 1) * rows]


def write_log(message, h, total):
    rows = message.shape[2] - EXTRA
    high = total.astype(bf16).astype(f32)
    middle = (total - high).astype(bf16).astype(f32)
    low = total - high - middle
    place = lax.broadcasted_iota(jnp.int32, (EXTRA, total.shape[1]), 0)
    tail = jnp.where(
        place == 0, high, jnp.where(place == 1, middle, jnp.where(place == 2, low, 0.0))
    )
    for k in range(message.shape[0]):
        message[k, h, rows:] = tail.astype(bf16)


def read_log(message, k, h):
    rows = message.shape[2] - EXTRA
    tail = message[k, h, rows:].astype(f32)
    return tail[0:1] + tail[1:2] + tail[2:3]


def upstream_kernel(
    grad, panel, gate, saved, cumulative, out_group, gate_grad, scan_grad, message, total
):
    step = pl.program_id(0)
    quarters, blocks, rows, columns = panel.shape
    weights = jnp.concatenate(
        [panel[:, b].reshape(quarters * rows, columns) for b in range(blocks)], axis=1
    )
    product = lax.dot_general(grad[...], weights, NT, preferred_element_type=f32)

    @pl.when(step == 0)
    def _():
        total[...] = product

    @pl.when(step > 0)
    def _():
        total[...] += product

    @pl.when(step == pl.num_programs(0) - 1)
    def _():
        upstream = total[...]
        value = gate[...].astype(f32)
        sig = jax.nn.sigmoid(value)
        gate_grad[...] = (
            upstream * saved[...].astype(f32) * sig * (1.0 + value * (1.0 - sig))
        ).astype(bf16)
        scan = (upstream * (value * sig)).astype(bf16)
        scan_grad[...] = scan
        heads = cumulative.shape[1]
        width = scan.shape[1] // heads
        weighted = scan.astype(f32) * by_head(jnp.exp(cumulative[...]), width)
        local = lax.dot_general(
            weighted.astype(bf16), out_group[...], TN, preferred_element_type=f32
        )
        states = local.shape[1]
        for h in range(heads):
            term = local[h * width : (h + 1) * width].astype(bf16)
            for k in range(message.shape[0]):
                message[k, h, :width] = term
            last = jnp.broadcast_to(cumulative[cumulative.shape[0] - 1 :, h : h + 1], (1, states))
            write_log(message, h, last)


def row_kernel(x_ref, received, message, in_row, tail_log):
    x = x_ref[0]
    ring, heads, rows, states = received.shape
    width = rows - EXTRA
    for h in range(heads):
        carry = jnp.zeros((width, states), f32)
        inside = carry
        logs = jnp.zeros((1, states), f32)
        tail = logs
        for j in reversed(range(ring)):
            log = read_log(received, j, h)
            inside = jnp.where(x == j, carry, inside)
            tail = jnp.where(x == j, logs, tail)
            carry = received[j, h, :width].astype(f32) + jnp.exp(log) * carry
            logs = logs + log
        in_row[h] = inside
        tail_log[h] = jnp.broadcast_to(tail, tail_log.shape[1:])
        for k in range(message.shape[0]):
            message[k, h, :width] = carry.astype(bf16)
        write_log(message, h, logs)


def inside_kernel(in_group, out_group, cumulative, turned, scan_grad, step_size, skip_gain, out):
    length, heads = cumulative.shape
    width = scan_grad.shape[1] // heads
    size = 128
    for start in range(0, length, size):
        here = slice(start, start + size)
        dots = lax.dot_general(
            in_group[here], out_group[start:], NT, preferred_element_type=f32
        )
        t = lax.broadcasted_iota(jnp.int32, dots.shape, 0)
        s = lax.broadcasted_iota(jnp.int32, dots.shape, 1)
        terms = []
        for h in range(heads):
            spread = turned[h : h + 1, start:] - cumulative[here, h : h + 1]
            factor = jnp.where(t <= s, jnp.exp(jnp.minimum(spread, 0.0)), 0.0)
            terms.append(
                jnp.dot(
                    (dots * factor).astype(bf16),
                    scan_grad[start:, h * width : (h + 1) * width],
                    preferred_element_type=f32,
                )
            )
        inside = jnp.concatenate(terms, axis=1)
        out[here] = by_head(step_size[here], width) * inside + by_head(
            jnp.broadcast_to(skip_gain[...], (size, heads)), width
        ) * scan_grad[here].astype(f32)


def carried_kernel(rows_z, z_ref, *refs):
    received = refs[: rows_z - 1]
    in_row, tail_log, in_group, cumulative, step_size, partial, out = refs[rows_z - 1 :]
    z = z_ref[0]
    _, heads, rows, states = received[0].shape
    width = rows - EXTRA
    length = cumulative.shape[0]
    terms = []
    for h in range(heads):
        carry = jnp.zeros((width, states), f32)
        for j in reversed(range(1, rows_z)):
            message = received[j - 1]
            term = message[0, h, :width].astype(f32)
            term = term + jnp.exp(read_log(message, 0, h)) * carry
            carry = jnp.where(z + j < rows_z, term, carry)
        carried = in_row[h] + jnp.exp(tail_log[h, 0:1]) * carry
        terms.append(
            lax.dot_general(in_group[...], carried.astype(bf16), NT, preferred_element_type=f32)
        )
    decay = jnp.exp(cumulative[length - 1 :] - cumulative[...])
    scale = by_head(step_size[...] * decay, width)
    out[...] = (partial[...] + scale * jnp.concatenate(terms, axis=1)).astype(bf16)


def cost(flops, bytes_accessed, transcendentals=0):
    return pl.CostEstimate(
        flops=flops, bytes_accessed=bytes_accessed, transcendentals=transcendentals
    )


def along_x(block, step):
    rows = lax.axis_size("seq")
    route = [(i, i // RING * RING + (i + step) % RING) for i in range(rows)]
    return lax.ppermute(block, "seq", route)


def along_z(block, step):
    size = lax.axis_size("seq")
    return lax.ppermute(block, "seq", [(i, (i + RING * step) % size) for i in range(size)])


def total_of(*terms):
    return sum(t.astype(f32) for t in terms).astype(bf16)


def to_group(blocks, groups):
    return lax.all_to_all(
        blocks, "seq", split_axis=0, concat_axis=0, tiled=True, axis_index_groups=groups
    )


def after(value, *others):
    return lax.optimization_barrier((value, *others))[0]


def on_device(
    out_grad,
    out_weight,
    gate_input,
    scan_output,
    step_size,
    log_decay,
    input_map,
    output_map,
    skip_gain,
):
    length, width = out_grad.shape
    heads_here = log_decay.shape[1]
    columns_here = gate_input.shape[1]
    head_width = columns_here // heads_here
    seq_size = lax.axis_size("seq")
    head_size = lax.axis_size("head")
    rows_z = seq_size // RING
    quarter = columns_here // RING
    column_block = width // head_size
    states = input_map.shape[2]
    message_rows = head_width + EXTRA
    me = lax.axis_index("seq")
    x = (me % RING).astype(jnp.int32)
    z = (me // RING).astype(jnp.int32)
    rings = [[r * RING + i for i in range(RING)] for r in range(rows_z)]
    steps = 2
    blocks = head_size // steps
    wide = blocks * column_block

    half = head_size // 2
    half_blocks = max(half // PART_STEPS, 1)
    part_steps = half // half_blocks

    def block_parts(which):
        wide_part = half_blocks * column_block
        return pl.pallas_call(
            functools.partial(part_kernel, 1.0 / math.sqrt(length * seq_size)),
            name="block_parts",
            grid=(part_steps,),
            in_specs=[
                SMEM,
                pl.BlockSpec((length, columns_here), lambda i: (0, 0)),
                pl.BlockSpec((length, columns_here), lambda i: (0, 0)),
                pl.BlockSpec((length, wide_part), lambda i: (0, i + which * part_steps)),
            ],
            out_specs=[pl.BlockSpec((half_blocks, quarter, column_block), lambda i: (i, 0, 0))]
            * RING,
            out_shape=[jax.ShapeDtypeStruct((half, quarter, column_block), bf16)] * RING,
            scratch_shapes=[
                pltpu.VMEM((columns_here, length), f32),
                pltpu.VMEM((columns_here, length), bf16),
            ],
            cost_estimate=cost(length * width * columns_here, length * width),
        )(x.reshape(1), gate_input, scan_output, out_grad)

    def sum_on_ring(parts, step):
        own, forth, opposite, back = parts if step == 1 else (parts[0], parts[3], parts[2], parts[1])
        passed = along_x(opposite, step)
        got = along_x(back, -step)
        return total_of(own, got, along_x(total_of(forth, passed), step))

    first = block_parts(0)
    second = block_parts(1)
    first_sum = sum_on_ring(first, 1)
    second_sum = sum_on_ring(second, -1)
    quarter_sum = jnp.concatenate(
        [
            total_of(part, along_z(part, 1), along_z(part, 2))
            for part in (first_sum, second_sum)
        ],
        axis=0,
    )

    group_index = lax.axis_index("head") * heads_here // (HEAD_COUNT // G)
    in_group = lax.dynamic_index_in_dim(input_map, group_index, 1, keepdims=False)
    out_group = lax.dynamic_index_in_dim(output_map, group_index, 1, keepdims=False)
    cumulative = jnp.cumsum(log_decay, axis=0)
    turned = cumulative.T

    weight_quarter = lax.dynamic_index_in_dim(
        after(out_weight, *second).reshape(head_size, RING, quarter, column_block),
        x,
        1,
        keepdims=False,
    )
    rows_quarter = lax.all_to_all(weight_quarter, "head", split_axis=0, concat_axis=0, tiled=True)
    rows_quarter, in_group, out_group, cumulative, turned, step_size, _, _ = lax.optimization_barrier(
        (
            rows_quarter,
            in_group,
            out_group,
            cumulative,
            turned,
            step_size,
            first_sum,
            second_sum,
        )
    )
    panel = to_group(jnp.broadcast_to(rows_quarter[None], (RING, *rows_quarter.shape)), rings)

    whole = lambda shape: pl.BlockSpec(shape, lambda i: (0,) * len(shape))
    panel_shape = (length, columns_here)
    gate_grad, scan_grad, message = pl.pallas_call(
        upstream_kernel,
        name="upstream",
        grid=(steps,),
        in_specs=[
            pl.BlockSpec((length, wide), lambda i: (0, i)),
            pl.BlockSpec((RING, blocks, quarter, column_block), lambda i: (0, i, 0, 0)),
            whole(panel_shape),
            whole(panel_shape),
            whole((length, heads_here)),
            whole((length, states)),
        ],
        out_specs=[
            whole(panel_shape),
            whole(panel_shape),
            whole((RING, heads_here, message_rows, states)),
        ],
        out_shape=[
            jax.ShapeDtypeStruct(panel_shape, bf16),
            jax.ShapeDtypeStruct(panel_shape, bf16),
            jax.ShapeDtypeStruct((RING, heads_here, message_rows, states), bf16),
        ],
        scratch_shapes=[pltpu.VMEM(panel_shape, f32)],
        cost_estimate=cost(2 * length * width * columns_here, 2 * length * width),
    )(out_grad, panel, gate_input, scan_output, cumulative, out_group)

    state = (heads_here, head_width, states)
    partial = pl.pallas_call(
        inside_kernel,
        name="inside",
        in_specs=[VMEM] * 7,
        out_specs=VMEM,
        out_shape=jax.ShapeDtypeStruct(panel_shape, f32),
        cost_estimate=cost(4 * 10**8, 2 * 10**6, 2 * length * length),
    )(
        in_group,
        out_group,
        cumulative,
        turned,
        scan_grad,
        step_size,
        skip_gain.reshape(1, heads_here),
    )
    by_place = after(to_group(message, rings), partial)
    row_message, in_row, tail_log = pl.pallas_call(
        row_kernel,
        name="row_scan",
        in_specs=[SMEM, VMEM],
        out_specs=[VMEM, VMEM, VMEM],
        out_shape=[
            jax.ShapeDtypeStruct((1, heads_here, message_rows, states), bf16),
            jax.ShapeDtypeStruct(state, f32),
            jax.ShapeDtypeStruct((heads_here, 8, states), f32),
        ],
        cost_estimate=cost(10**6, 10**6),
    )(x.reshape(1), by_place)
    from_rows = [
        lax.ppermute(
            row_message, "seq", [(i + j * RING, i) for i in range(seq_size - j * RING)]
        )
        for j in range(1, rows_z)
    ]
    input_grad = pl.pallas_call(
        functools.partial(carried_kernel, rows_z),
        name="carried",
        in_specs=[SMEM] + [VMEM] * (5 + rows_z),
        out_specs=VMEM,
        out_shape=jax.ShapeDtypeStruct(panel_shape, bf16),
        cost_estimate=cost(10**8, 10**6),
    )(z.reshape(1), *from_rows, in_row, tail_log, in_group, cumulative, step_size, partial)

    pieces = lax.all_to_all(quarter_sum, "head", split_axis=0, concat_axis=0, tiled=True)
    all_quarters = to_group(jnp.broadcast_to(pieces[None], (RING, *pieces.shape)), rings)
    weight_grad = jnp.transpose(all_quarters, (1, 0, 2, 3)).reshape(
        head_size * columns_here, column_block
    )
    return (input_grad, gate_grad, weight_grad)


def solution(mesh):
    in_specs = (
        P("seq", None),
        P(None, "head"),
        P("seq", "head"),
        P("seq", "head"),
        P("seq", "head"),
        P("seq", "head"),
        P("seq", None, None),
        P("seq", None, None),
        P("head"),
    )
    out_specs = (P("seq", "head"), P("seq", "head"), P(None, "head"))
    return jax.shard_map(
        on_device, mesh=mesh, in_specs=in_specs, out_specs=out_specs, check_vma=False
    )
```

```python
import functools
import math

import jax
import jax.numpy as jnp
from jax import lax
from jax.experimental import pallas as pl
from jax.experimental.pallas import tpu as pltpu
from jax.sharding import PartitionSpec as P

HEAD_COUNT = 128
G = 4
RING = 4
EXTRA = 16

f32 = jnp.float32
bf16 = jnp.bfloat16
VMEM = pl.BlockSpec(memory_space=pltpu.VMEM)
SMEM = pl.BlockSpec(memory_space=pltpu.SMEM)
NT = (((1,), (1,)), ((), ()))
TN = (((0,), (0,)), ((), ()))


def by_head(columns, width):
    rows, heads = columns.shape
    head = lax.broadcasted_iota(jnp.int32, (rows, heads * width), 1) // width
    out = jnp.broadcast_to(columns[:, :1], (rows, heads * width))
    for h in range(1, heads):
        out = jnp.where(head == h, columns[:, h : h + 1], out)
    return out


def part_kernel(scale, x_ref, gate, saved, grad, *rest):
    outs, turned, ordered = rest[: 2 * RING], rest[2 * RING], rest[2 * RING + 1]
    blocks, rows, columns = outs[0].shape

    @pl.when(pl.program_id(0) == 0)
    def _():
        value = gate[...].astype(f32)
        gated = saved[...].astype(f32) * (value * jax.nn.sigmoid(value))
        turned[...] = gated.T
        for j in range(RING):
            start = pl.multiple_of((x_ref[0] + j) % RING * rows, rows)
            ordered[j * rows : (j + 1) * rows] = turned[pl.ds(start, rows)].astype(bf16)

    product = jnp.dot(ordered[...], grad[...], preferred_element_type=f32) * scale
    for which in range(2):

        @pl.when(pl.program_id(0) == which)
        def _():
            for b in range(blocks):
                piece = product[:, b * columns : (b + 1) * columns].astype(bf16)
                for j in range(RING):
                    outs[which * RING + j][b] = piece[j * rows : (j + 1) * rows]


def window_starts(rows_z, half):
    window = -(-half // rows_z)
    return window, [k * (half - window) // (rows_z - 1) for k in range(rows_z)]


def window_of(rows_z, half, k):
    starts = window_starts(rows_z, half)[1]
    k = k % rows_z
    start = jnp.int32(starts[0])
    for i in range(1, rows_z):
        start = jnp.where(k == i, starts[i], start)
    return start


def ring_sum_kernel(rows_z, z_ref, own, got, more, *outs):
    half, window = own.shape[0], outs[0].shape[0]
    for j in range(rows_z):
        rows = pl.ds(window_of(rows_z, half, z_ref[0] + j), window)
        outs[j][...] = (
            own[rows].astype(f32) + got[rows].astype(f32) + more[rows].astype(f32)
        ).astype(bf16)


def assemble_kernel(rows_z, z_ref, *refs):
    pieces, out = refs[:-1], refs[-1]
    half = out.shape[0] // 2
    window = pieces[0].shape[0]
    for which in range(2):
        for j in range(rows_z):
            start = window_of(rows_z, half, z_ref[0] + j) + which * half
            out[pl.ds(start, window)] = pieces[which * rows_z + j][...]


def order_kernel(quarters, out):
    for q in range(quarters.shape[0]):
        out[:, q] = quarters[q]


def write_log(message, h, total):
    rows = message.shape[2] - EXTRA
    high = total.astype(bf16).astype(f32)
    middle = (total - high).astype(bf16).astype(f32)
    low = total - high - middle
    place = lax.broadcasted_iota(jnp.int32, (EXTRA, total.shape[1]), 0)
    tail = jnp.where(
        place == 0, high, jnp.where(place == 1, middle, jnp.where(place == 2, low, 0.0))
    )
    for k in range(message.shape[0]):
        message[k, h, rows:] = tail.astype(bf16)


def read_log(message, k, h):
    rows = message.shape[2] - EXTRA
    tail = message[k, h, rows:].astype(f32)
    return tail[0:1] + tail[1:2] + tail[2:3]


def upstream_kernel(
    grad, panel, gate, saved, cumulative, out_group, gate_grad, scan_grad, message, total
):
    step = pl.program_id(0)
    quarters, blocks, rows, columns = panel.shape
    weights = jnp.concatenate(
        [panel[:, b].reshape(quarters * rows, columns) for b in range(blocks)], axis=1
    )
    product = lax.dot_general(grad[...], weights, NT, preferred_element_type=f32)

    @pl.when(step == 0)
    def _():
        total[...] = product

    @pl.when(step > 0)
    def _():
        total[...] += product

    @pl.when(step == pl.num_programs(0) - 1)
    def _():
        upstream = total[...]
        value = gate[...].astype(f32)
        sig = jax.nn.sigmoid(value)
        gate_grad[...] = (
            upstream * saved[...].astype(f32) * sig * (1.0 + value * (1.0 - sig))
        ).astype(bf16)
        scan = (upstream * (value * sig)).astype(bf16)
        scan_grad[...] = scan
        heads = cumulative.shape[1]
        width = scan.shape[1] // heads
        weighted = scan.astype(f32) * by_head(jnp.exp(cumulative[...]), width)
        local = lax.dot_general(
            weighted.astype(bf16), out_group[...], TN, preferred_element_type=f32
        )
        states = local.shape[1]
        for h in range(heads):
            term = local[h * width : (h + 1) * width].astype(bf16)
            for k in range(message.shape[0]):
                message[k, h, :width] = term
            last = jnp.broadcast_to(cumulative[cumulative.shape[0] - 1 :, h : h + 1], (1, states))
            write_log(message, h, last)


def row_kernel(x_ref, *refs):
    received, (message, in_row, tail_log) = refs[:RING], refs[RING:]
    x = x_ref[0]
    _, heads, rows, states = message.shape
    width = rows - EXTRA
    for h in range(heads):
        carry = jnp.zeros((width, states), f32)
        logs = jnp.zeros((1, states), f32)

        def further(j, keep, carry, logs):
            log = read_log(received[j], 0, h)
            term = received[j][0, h, :width].astype(f32) + jnp.exp(log) * carry
            return jnp.where(keep, term, carry), jnp.where(keep, logs + log, logs)

        for j in reversed(range(1, RING)):
            carry, logs = further(j, x + j < RING, carry, logs)
        in_row[h] = carry
        tail_log[h] = jnp.broadcast_to(logs, tail_log.shape[1:])
        carry, logs = further(0, x >= 0, carry, logs)
        for j in reversed(range(1, RING)):
            carry, logs = further(j, x + j >= RING, carry, logs)
        message[0, h, :width] = carry.astype(bf16)
        write_log(message, h, logs)


def inside_kernel(in_group, out_group, cumulative, turned, scan_grad, step_size, skip_gain, out):
    length, heads = cumulative.shape
    width = scan_grad.shape[1] // heads
    size = 128
    for start in range(0, length, size):
        here = slice(start, start + size)
        dots = lax.dot_general(
            in_group[here], out_group[start:], NT, preferred_element_type=f32
        )
        t = lax.broadcasted_iota(jnp.int32, dots.shape, 0)
        s = lax.broadcasted_iota(jnp.int32, dots.shape, 1)
        terms = []
        for h in range(heads):
            spread = turned[h : h + 1, start:] - cumulative[here, h : h + 1]
            factor = jnp.where(t <= s, jnp.exp(jnp.minimum(spread, 0.0)), 0.0)
            terms.append(
                jnp.dot(
                    (dots * factor).astype(bf16),
                    scan_grad[start:, h * width : (h + 1) * width],
                    preferred_element_type=f32,
                )
            )
        inside = jnp.concatenate(terms, axis=1)
        out[here] = by_head(step_size[here], width) * inside + by_head(
            jnp.broadcast_to(skip_gain[...], (size, heads)), width
        ) * scan_grad[here].astype(f32)


def carried_kernel(rows_z, z_ref, *refs):
    received = refs[: rows_z - 1]
    in_row, tail_log, in_group, cumulative, step_size, partial, out = refs[rows_z - 1 :]
    z = z_ref[0]
    _, heads, rows, states = received[0].shape
    width = rows - EXTRA
    length = cumulative.shape[0]
    terms = []
    for h in range(heads):
        carry = jnp.zeros((width, states), f32)
        for j in reversed(range(1, rows_z)):
            message = received[j - 1]
            term = message[0, h, :width].astype(f32)
            term = term + jnp.exp(read_log(message, 0, h)) * carry
            carry = jnp.where(z + j < rows_z, term, carry)
        carried = in_row[h] + jnp.exp(tail_log[h, 0:1]) * carry
        terms.append(
            lax.dot_general(in_group[...], carried.astype(bf16), NT, preferred_element_type=f32)
        )
    decay = jnp.exp(cumulative[length - 1 :] - cumulative[...])
    scale = by_head(step_size[...] * decay, width)
    out[...] = (partial[...] + scale * jnp.concatenate(terms, axis=1)).astype(bf16)


def cost(flops, bytes_accessed, transcendentals=0):
    return pl.CostEstimate(
        flops=flops, bytes_accessed=bytes_accessed, transcendentals=transcendentals
    )


def along_x(block, step):
    rows = lax.axis_size("seq")
    route = [(i, i // RING * RING + (i + step) % RING) for i in range(rows)]
    return lax.ppermute(block, "seq", route)


def along_z(block, step):
    size = lax.axis_size("seq")
    return lax.ppermute(block, "seq", [(i, (i + RING * step) % size) for i in range(size)])


def total_of(*terms):
    return sum(t.astype(f32) for t in terms).astype(bf16)


def to_group(blocks, groups):
    return lax.all_to_all(
        blocks, "seq", split_axis=0, concat_axis=0, tiled=True, axis_index_groups=groups
    )


def after(value, *others):
    return lax.optimization_barrier((value, *others))[0]


def on_device(
    out_grad,
    out_weight,
    gate_input,
    scan_output,
    step_size,
    log_decay,
    input_map,
    output_map,
    skip_gain,
):
    length, width = out_grad.shape
    heads_here = log_decay.shape[1]
    columns_here = gate_input.shape[1]
    head_width = columns_here // heads_here
    seq_size = lax.axis_size("seq")
    head_size = lax.axis_size("head")
    rows_z = seq_size // RING
    quarter = columns_here // RING
    column_block = width // head_size
    states = input_map.shape[2]
    message_rows = head_width + EXTRA
    me = lax.axis_index("seq")
    x = (me % RING).astype(jnp.int32)
    z = (me // RING).astype(jnp.int32)
    rings = [[r * RING + i for i in range(RING)] for r in range(rows_z)]
    steps = 2
    blocks = head_size // steps
    wide = blocks * column_block

    half = head_size // 2
    whole = lambda shape: pl.BlockSpec(shape, lambda *_: (0,) * len(shape))
    half_shape = (half, quarter, column_block)
    z_place = z.reshape(1)
    parts = pl.pallas_call(
        functools.partial(part_kernel, 1.0 / math.sqrt(length * seq_size)),
        name="block_parts",
        grid=(2,),
        in_specs=[
            SMEM,
            whole((length, columns_here)),
            whole((length, columns_here)),
            pl.BlockSpec((length, half * column_block), lambda i: (0, i)),
        ],
        out_specs=[whole(half_shape)] * (2 * RING),
        out_shape=[jax.ShapeDtypeStruct(half_shape, bf16)] * (2 * RING),
        scratch_shapes=[
            pltpu.VMEM((columns_here, length), f32),
            pltpu.VMEM((columns_here, length), bf16),
        ],
        cost_estimate=cost(2 * length * width * columns_here, 2 * length * width),
    )(x.reshape(1), gate_input, scan_output, out_grad)
    own_a, next_a, far_a, back_a, own_b, back_b, far_b, next_b = parts
    passed_a = along_x(far_a, 1)
    passed_b = along_x(far_b, -1)
    got_b = along_x(back_b, 1)
    got_a = along_x(back_a, -1)
    more_a = along_x(total_of(next_a, passed_a), 1)
    more_b = along_x(total_of(next_b, passed_b), -1)
    window = window_starts(rows_z, half)[0]
    window_shape = (window, quarter, column_block)

    def windows_of(*terms):
        return pl.pallas_call(
            functools.partial(ring_sum_kernel, rows_z),
            name="ring_sum",
            in_specs=[SMEM] + [VMEM] * 3,
            out_specs=[VMEM] * rows_z,
            out_shape=[jax.ShapeDtypeStruct(window_shape, bf16)] * rows_z,
            cost_estimate=cost(10**6, 2 * 10**6),
        )(z_place, *terms)

    windows_a = windows_of(own_a, got_a, more_a)
    windows_b = windows_of(own_b, got_b, more_b)
    reduced = [
        total_of(w[0], *(along_z(w[j], j) for j in range(1, rows_z)))
        for w in (windows_a, windows_b)
    ]
    gathered = [r if j == 0 else along_z(r, -j) for r in reduced for j in range(rows_z)]

    group_index = lax.axis_index("head") * heads_here // (HEAD_COUNT // G)
    in_group = lax.dynamic_index_in_dim(input_map, group_index, 1, keepdims=False)
    out_group = lax.dynamic_index_in_dim(output_map, group_index, 1, keepdims=False)
    cumulative = jnp.cumsum(log_decay, axis=0)
    turned = cumulative.T

    weight_quarter = lax.dynamic_index_in_dim(
        out_weight.reshape(head_size, RING, quarter, column_block),
        x,
        1,
        keepdims=False,
    )
    rows_quarter = lax.all_to_all(weight_quarter, "head", split_axis=0, concat_axis=0, tiled=True)
    rows_quarter, in_group, out_group, cumulative, turned, step_size, _, _ = lax.optimization_barrier(
        (
            rows_quarter,
            in_group,
            out_group,
            cumulative,
            turned,
            step_size,
            windows_a[0],
            windows_b[0],
        )
    )
    panel = to_group(jnp.broadcast_to(rows_quarter[None], (RING, *rows_quarter.shape)), rings)
    panel = after(panel, *reduced)

    panel_shape = (length, columns_here)
    gate_grad, scan_grad, message = pl.pallas_call(
        upstream_kernel,
        name="upstream",
        grid=(steps,),
        in_specs=[
            pl.BlockSpec((length, wide), lambda i: (0, i)),
            pl.BlockSpec((RING, blocks, quarter, column_block), lambda i: (0, i, 0, 0)),
            whole(panel_shape),
            whole(panel_shape),
            whole((length, heads_here)),
            whole((length, states)),
        ],
        out_specs=[
            whole(panel_shape),
            whole(panel_shape),
            whole((1, heads_here, message_rows, states)),
        ],
        out_shape=[
            jax.ShapeDtypeStruct(panel_shape, bf16),
            jax.ShapeDtypeStruct(panel_shape, bf16),
            jax.ShapeDtypeStruct((1, heads_here, message_rows, states), bf16),
        ],
        scratch_shapes=[pltpu.VMEM(panel_shape, f32)],
        cost_estimate=cost(2 * length * width * columns_here, 2 * length * width),
    )(out_grad, panel, gate_input, scan_output, cumulative, out_group)

    state = (heads_here, head_width, states)
    partial = pl.pallas_call(
        inside_kernel,
        name="inside",
        in_specs=[VMEM] * 7,
        out_specs=VMEM,
        out_shape=jax.ShapeDtypeStruct(panel_shape, f32),
        cost_estimate=cost(4 * 10**8, 2 * 10**6, 2 * length * length),
    )(
        in_group,
        out_group,
        cumulative,
        turned,
        scan_grad,
        step_size,
        skip_gain.reshape(1, heads_here),
    )
    on_ring = [message if j == 0 else along_x(message, -j) for j in range(RING)]
    row_message, in_row, tail_log = pl.pallas_call(
        row_kernel,
        name="row_scan",
        in_specs=[SMEM] + [VMEM] * RING,
        out_specs=[VMEM, VMEM, VMEM],
        out_shape=[
            jax.ShapeDtypeStruct((1, heads_here, message_rows, states), bf16),
            jax.ShapeDtypeStruct(state, f32),
            jax.ShapeDtypeStruct((heads_here, 8, states), f32),
        ],
        cost_estimate=cost(10**6, 10**6),
    )(x.reshape(1), *on_ring)
    from_rows = [
        lax.ppermute(
            row_message, "seq", [(i + j * RING, i) for i in range(seq_size - j * RING)]
        )
        for j in range(1, rows_z)
    ]
    input_grad = pl.pallas_call(
        functools.partial(carried_kernel, rows_z),
        name="carried",
        in_specs=[SMEM] + [VMEM] * (5 + rows_z),
        out_specs=VMEM,
        out_shape=jax.ShapeDtypeStruct(panel_shape, bf16),
        cost_estimate=cost(10**8, 10**6),
    )(z.reshape(1), *from_rows, in_row, tail_log, in_group, cumulative, step_size, partial)

    quarter_sum = pl.pallas_call(
        functools.partial(assemble_kernel, rows_z),
        name="assemble",
        in_specs=[SMEM] + [VMEM] * (2 * rows_z),
        out_specs=VMEM,
        out_shape=jax.ShapeDtypeStruct((head_size, quarter, column_block), bf16),
        cost_estimate=cost(10**5, 10**6),
    )(z_place, *gathered[:-1], after(gathered[-1], message))
    pieces = lax.all_to_all(quarter_sum, "head", split_axis=0, concat_axis=0, tiled=True)
    pieces = after(pieces, row_message, partial)
    all_quarters = to_group(jnp.broadcast_to(pieces[None], (RING, *pieces.shape)), rings)
    chunk = max(head_size // 4, 1)
    weight_grad = pl.pallas_call(
        order_kernel,
        name="order",
        grid=(head_size // chunk,),
        in_specs=[pl.BlockSpec((RING, chunk, quarter, column_block), lambda i: (0, i, 0, 0))],
        out_specs=pl.BlockSpec((chunk, RING, quarter, column_block), lambda i: (i, 0, 0, 0)),
        out_shape=jax.ShapeDtypeStruct((head_size, RING, quarter, column_block), bf16),
        cost_estimate=cost(10**5, 4 * 10**6),
    )(all_quarters).reshape(head_size * columns_here, column_block)
    return (input_grad, gate_grad, weight_grad)


def solution(mesh):
    in_specs = (
        P("seq", None),
        P(None, "head"),
        P("seq", "head"),
        P("seq", "head"),
        P("seq", "head"),
        P("seq", "head"),
        P("seq", None, None),
        P("seq", None, None),
        P("head"),
    )
    out_specs = (P("seq", "head"), P("seq", "head"), P(None, "head"))
    return jax.shard_map(
        on_device, mesh=mesh, in_specs=in_specs, out_specs=out_specs, check_vma=False
    )
```

```python
import functools
import math

import jax
import jax.numpy as jnp
from jax import lax
from jax.experimental import pallas as pl
from jax.experimental.pallas import tpu as pltpu
from jax.sharding import PartitionSpec as P

HEAD_COUNT = 128
G = 4
RING = 4
EXTRA = 16

f32 = jnp.float32
bf16 = jnp.bfloat16
VMEM = pl.BlockSpec(memory_space=pltpu.VMEM)
SMEM = pl.BlockSpec(memory_space=pltpu.SMEM)
NT = (((1,), (1,)), ((), ()))
TN = (((0,), (0,)), ((), ()))


def by_head(columns, width):
    rows, heads = columns.shape
    head = lax.broadcasted_iota(jnp.int32, (rows, heads * width), 1) // width
    out = jnp.broadcast_to(columns[:, :1], (rows, heads * width))
    for h in range(1, heads):
        out = jnp.where(head == h, columns[:, h : h + 1], out)
    return out


def part_kernel(scale, x_ref, gate, saved, grad, *rest):
    outs, turned, ordered = rest[:RING], rest[RING], rest[RING + 1]
    blocks, rows, columns = outs[0].shape

    @pl.when(pl.program_id(0) == 0)
    def _():
        value = gate[...].astype(f32)
        gated = saved[...].astype(f32) * (value * jax.nn.sigmoid(value))
        turned[...] = gated.T
        for j in range(RING):
            start = pl.multiple_of((x_ref[0] + j) % RING * rows, rows)
            ordered[j * rows : (j + 1) * rows] = turned[pl.ds(start, rows)].astype(bf16)

    product = jnp.dot(ordered[...], grad[...], preferred_element_type=f32) * scale
    for b in range(blocks):
        piece = product[:, b * columns : (b + 1) * columns].astype(bf16)
        for j in range(RING):
            outs[j][b] = piece[j * rows : (j + 1) * rows]


def ring_sum_kernel(starts, *refs):
    terms, out = refs[:-1], refs[-1]
    window = out.shape[1]
    for k, start in enumerate(starts):
        rows = slice(start, start + window)
        out[k] = sum(t[rows].astype(f32) for t in terms).astype(bf16)


def line_sum_kernel(windows, out):
    total = sum(windows[k].astype(f32) for k in range(windows.shape[0])).astype(bf16)
    for k in range(out.shape[0]):
        out[k] = total


def assemble_kernel(starts, windows, out):
    ends = starts[1:] + [out.shape[0]]
    for k, (start, end) in enumerate(zip(starts, ends)):
        out[start:end] = windows[k, : end - start]


def order_kernel(quarters, out):
    for q in range(quarters.shape[0]):
        out[:, q] = quarters[q]


def write_log(message, h, total):
    rows = message.shape[2] - EXTRA
    high = total.astype(bf16).astype(f32)
    middle = (total - high).astype(bf16).astype(f32)
    low = total - high - middle
    place = lax.broadcasted_iota(jnp.int32, (EXTRA, total.shape[1]), 0)
    tail = jnp.where(
        place == 0, high, jnp.where(place == 1, middle, jnp.where(place == 2, low, 0.0))
    )
    for k in range(message.shape[0]):
        message[k, h, rows:] = tail.astype(bf16)


def read_log(message, k, h):
    rows = message.shape[2] - EXTRA
    tail = message[k, h, rows:].astype(f32)
    return tail[0:1] + tail[1:2] + tail[2:3]


def upstream_kernel(x_ref, grad, *refs):
    panels = refs[:RING]
    gate, saved, cumulative, out_group, gate_grad, scan_grad, message, total = refs[RING:]
    step = pl.program_id(0)
    blocks, rows, columns = panels[0].shape
    weights = jnp.concatenate(
        [jnp.concatenate([p[b] for p in panels], axis=0) for b in range(blocks)], axis=1
    )
    product = lax.dot_general(grad[...], weights, NT, preferred_element_type=f32)

    @pl.when(step == 0)
    def _():
        total[...] = product

    @pl.when(step > 0)
    def _():
        total[...] += product

    @pl.when(step == pl.num_programs(0) - 1)
    def _():
        upstream = pltpu.roll(total[...], x_ref[0] * rows, 1)
        value = gate[...].astype(f32)
        sig = jax.nn.sigmoid(value)
        gate_grad[...] = (
            upstream * saved[...].astype(f32) * sig * (1.0 + value * (1.0 - sig))
        ).astype(bf16)
        scan = (upstream * (value * sig)).astype(bf16)
        scan_grad[...] = scan
        heads = cumulative.shape[1]
        width = scan.shape[1] // heads
        weighted = scan.astype(f32) * by_head(jnp.exp(cumulative[...]), width)
        local = lax.dot_general(
            weighted.astype(bf16), out_group[...], TN, preferred_element_type=f32
        )
        states = local.shape[1]
        for h in range(heads):
            term = local[h * width : (h + 1) * width].astype(bf16)
            for k in range(message.shape[0]):
                message[k, h, :width] = term
            last = jnp.broadcast_to(cumulative[cumulative.shape[0] - 1 :, h : h + 1], (1, states))
            write_log(message, h, last)


def row_kernel(x_ref, *refs):
    received, (message, in_row, tail_log) = refs[:RING], refs[RING:]
    x = x_ref[0]
    _, heads, rows, states = message.shape
    width = rows - EXTRA
    for h in range(heads):
        carry = jnp.zeros((width, states), f32)
        logs = jnp.zeros((1, states), f32)

        def further(j, keep, carry, logs):
            log = read_log(received[j], 0, h)
            term = received[j][0, h, :width].astype(f32) + jnp.exp(log) * carry
            return jnp.where(keep, term, carry), jnp.where(keep, logs + log, logs)

        for j in reversed(range(1, RING)):
            carry, logs = further(j, x + j < RING, carry, logs)
        in_row[h] = carry
        tail_log[h] = jnp.broadcast_to(logs, tail_log.shape[1:])
        carry, logs = further(0, x >= 0, carry, logs)
        for j in reversed(range(1, RING)):
            carry, logs = further(j, x + j >= RING, carry, logs)
        message[0, h, :width] = carry.astype(bf16)
        write_log(message, h, logs)


def inside_kernel(in_group, out_group, cumulative, turned, scan_grad, step_size, skip_gain, out):
    length, heads = cumulative.shape
    width = scan_grad.shape[1] // heads
    size = 128
    for start in range(0, length, size):
        here = slice(start, start + size)
        dots = lax.dot_general(
            in_group[here], out_group[start:], NT, preferred_element_type=f32
        )
        t = lax.broadcasted_iota(jnp.int32, dots.shape, 0)
        s = lax.broadcasted_iota(jnp.int32, dots.shape, 1)
        terms = []
        for h in range(heads):
            spread = turned[h : h + 1, start:] - cumulative[here, h : h + 1]
            factor = jnp.where(t <= s, jnp.exp(jnp.minimum(spread, 0.0)), 0.0)
            terms.append(
                jnp.dot(
                    (dots * factor).astype(bf16),
                    scan_grad[start:, h * width : (h + 1) * width],
                    preferred_element_type=f32,
                )
            )
        inside = jnp.concatenate(terms, axis=1)
        out[here] = by_head(step_size[here], width) * inside + by_head(
            jnp.broadcast_to(skip_gain[...], (size, heads)), width
        ) * scan_grad[here].astype(f32)


def carried_kernel(rows_z, z_ref, *refs):
    received = refs[: rows_z - 1]
    in_row, tail_log, in_group, cumulative, step_size, partial, out = refs[rows_z - 1 :]
    z = z_ref[0]
    _, heads, rows, states = received[0].shape
    width = rows - EXTRA
    length = cumulative.shape[0]
    terms = []
    for h in range(heads):
        carry = jnp.zeros((width, states), f32)
        for j in reversed(range(1, rows_z)):
            message = received[j - 1]
            term = message[0, h, :width].astype(f32)
            term = term + jnp.exp(read_log(message, 0, h)) * carry
            carry = jnp.where(z + j < rows_z, term, carry)
        carried = in_row[h] + jnp.exp(tail_log[h, 0:1]) * carry
        terms.append(
            lax.dot_general(in_group[...], carried.astype(bf16), NT, preferred_element_type=f32)
        )
    decay = jnp.exp(cumulative[length - 1 :] - cumulative[...])
    scale = by_head(step_size[...] * decay, width)
    out[...] = (partial[...] + scale * jnp.concatenate(terms, axis=1)).astype(bf16)


def cost(flops, bytes_accessed, transcendentals=0):
    return pl.CostEstimate(
        flops=flops, bytes_accessed=bytes_accessed, transcendentals=transcendentals
    )


def along_x(block, step):
    rows = lax.axis_size("seq")
    route = [(i, i // RING * RING + (i + step) % RING) for i in range(rows)]
    return lax.ppermute(block, "seq", route)


def to_group(blocks, groups):
    return lax.all_to_all(
        blocks, "seq", split_axis=0, concat_axis=0, tiled=True, axis_index_groups=groups
    )


def after(value, *others):
    return lax.optimization_barrier((value, *others))[0]


def on_device(
    out_grad,
    out_weight,
    gate_input,
    scan_output,
    step_size,
    log_decay,
    input_map,
    output_map,
    skip_gain,
):
    length, width = out_grad.shape
    heads_here = log_decay.shape[1]
    columns_here = gate_input.shape[1]
    head_width = columns_here // heads_here
    seq_size = lax.axis_size("seq")
    head_size = lax.axis_size("head")
    rows_z = seq_size // RING
    quarter = columns_here // RING
    column_block = width // head_size
    states = input_map.shape[2]
    message_rows = head_width + EXTRA
    me = lax.axis_index("seq")
    x = (me % RING).astype(jnp.int32)
    z = (me // RING).astype(jnp.int32)
    rings = [[r * RING + i for i in range(RING)] for r in range(rows_z)]
    lines = [[r * RING + i for r in range(rows_z)] for i in range(RING)]
    steps = 2
    blocks = head_size // steps
    wide = blocks * column_block

    weight_quarter = lax.dynamic_index_in_dim(
        out_weight.reshape(head_size, RING, quarter, column_block),
        x,
        1,
        keepdims=False,
    )
    rows_quarter = lax.all_to_all(weight_quarter, "head", split_axis=0, concat_axis=0, tiled=True)

    group_index = lax.axis_index("head") * heads_here // (HEAD_COUNT // G)
    in_group = lax.dynamic_index_in_dim(input_map, group_index, 1, keepdims=False)
    out_group = lax.dynamic_index_in_dim(output_map, group_index, 1, keepdims=False)
    cumulative = jnp.cumsum(log_decay, axis=0)
    turned = cumulative.T

    half = head_size // 2
    whole = lambda shape: pl.BlockSpec(shape, lambda *_: (0,) * len(shape))
    block_shape = (half, quarter, column_block)
    quarter_shape = (head_size, quarter, column_block)
    x_place = x.reshape(1)
    own, forth, opposite, back = pl.pallas_call(
        functools.partial(part_kernel, 1.0 / math.sqrt(length * seq_size)),
        name="block_parts",
        grid=(2,),
        in_specs=[
            SMEM,
            whole((length, columns_here)),
            whole((length, columns_here)),
            pl.BlockSpec((length, half * column_block), lambda i: (0, i)),
        ],
        out_specs=[pl.BlockSpec(block_shape, lambda i: (i, 0, 0))] * RING,
        out_shape=[jax.ShapeDtypeStruct(quarter_shape, bf16)] * RING,
        scratch_shapes=[
            pltpu.VMEM((columns_here, length), f32),
            pltpu.VMEM((columns_here, length), bf16),
        ],
        cost_estimate=cost(2 * length * width * columns_here, 2 * length * width),
    )(x_place, gate_input, scan_output, out_grad)
    own, rows_quarter, in_group, out_group, cumulative, turned, step_size = lax.optimization_barrier(
        (own, rows_quarter, in_group, out_group, cumulative, turned, step_size)
    )
    window = -(-head_size // rows_z)
    starts = [k * (head_size - window) // (rows_z - 1) for k in range(rows_z)]
    windows_shape = jax.ShapeDtypeStruct((rows_z, window, quarter, column_block), bf16)
    windows = pl.pallas_call(
        functools.partial(ring_sum_kernel, starts),
        name="ring_sum",
        in_specs=[VMEM] * RING,
        out_specs=VMEM,
        out_shape=windows_shape,
        cost_estimate=cost(10**6, 4 * 10**6),
    )(own, along_x(opposite, 2), along_x(forth, 1), along_x(back, -1))
    windows, rows_quarter = lax.optimization_barrier((windows, rows_quarter))
    panels = [
        rows_quarter,
        along_x(rows_quarter, -1),
        along_x(rows_quarter, 2),
        along_x(rows_quarter, 1),
    ]
    from_line, panels = lax.optimization_barrier((to_group(windows, lines), panels))
    reduced = pl.pallas_call(
        line_sum_kernel,
        name="line_sum",
        in_specs=[VMEM],
        out_specs=VMEM,
        out_shape=windows_shape,
        cost_estimate=cost(10**6, 2 * 10**6),
    )(from_line)
    panels, _ = lax.optimization_barrier((panels, reduced))
    gathered = to_group(reduced, lines)


    panel_shape = (length, columns_here)
    gate_grad, scan_grad, message = pl.pallas_call(
        upstream_kernel,
        name="upstream",
        grid=(steps,),
        in_specs=[
            SMEM,
            pl.BlockSpec((length, wide), lambda i: (0, i)),
            *[pl.BlockSpec((blocks, quarter, column_block), lambda i: (i, 0, 0))] * RING,
            whole(panel_shape),
            whole(panel_shape),
            whole((length, heads_here)),
            whole((length, states)),
        ],
        out_specs=[
            whole(panel_shape),
            whole(panel_shape),
            whole((1, heads_here, message_rows, states)),
        ],
        out_shape=[
            jax.ShapeDtypeStruct(panel_shape, bf16),
            jax.ShapeDtypeStruct(panel_shape, bf16),
            jax.ShapeDtypeStruct((1, heads_here, message_rows, states), bf16),
        ],
        scratch_shapes=[pltpu.VMEM(panel_shape, f32)],
        cost_estimate=cost(2 * length * width * columns_here, 2 * length * width),
    )(x_place, out_grad, *panels, gate_input, scan_output, cumulative, out_group)

    state = (heads_here, head_width, states)
    partial = pl.pallas_call(
        inside_kernel,
        name="inside",
        in_specs=[VMEM] * 7,
        out_specs=VMEM,
        out_shape=jax.ShapeDtypeStruct(panel_shape, f32),
        cost_estimate=cost(4 * 10**8, 2 * 10**6, 2 * length * length),
    )(
        in_group,
        out_group,
        cumulative,
        turned,
        scan_grad,
        step_size,
        skip_gain.reshape(1, heads_here),
    )
    on_ring = [message if j == 0 else along_x(message, -j) for j in range(RING)]
    row_message, in_row, tail_log = pl.pallas_call(
        row_kernel,
        name="row_scan",
        in_specs=[SMEM] + [VMEM] * RING,
        out_specs=[VMEM, VMEM, VMEM],
        out_shape=[
            jax.ShapeDtypeStruct((1, heads_here, message_rows, states), bf16),
            jax.ShapeDtypeStruct(state, f32),
            jax.ShapeDtypeStruct((heads_here, 8, states), f32),
        ],
        cost_estimate=cost(10**6, 10**6),
    )(x_place, *on_ring)
    from_rows = [
        lax.ppermute(
            row_message, "seq", [(i + j * RING, i) for i in range(seq_size - j * RING)]
        )
        for j in range(1, rows_z)
    ]
    input_grad = pl.pallas_call(
        functools.partial(carried_kernel, rows_z),
        name="carried",
        in_specs=[SMEM] + [VMEM] * (5 + rows_z),
        out_specs=VMEM,
        out_shape=jax.ShapeDtypeStruct(panel_shape, bf16),
        cost_estimate=cost(10**8, 10**6),
    )(z.reshape(1), *from_rows, in_row, tail_log, in_group, cumulative, step_size, partial)

    quarter_sum = pl.pallas_call(
        functools.partial(assemble_kernel, starts),
        name="assemble",
        in_specs=[VMEM],
        out_specs=VMEM,
        out_shape=jax.ShapeDtypeStruct(quarter_shape, bf16),
        cost_estimate=cost(10**5, 10**6),
    )(after(gathered, message))
    pieces = lax.all_to_all(quarter_sum, "head", split_axis=0, concat_axis=0, tiled=True)
    pieces = after(pieces, row_message, partial)
    all_quarters = to_group(jnp.broadcast_to(pieces[None], (RING, *pieces.shape)), rings)
    chunk = max(head_size // 4, 1)
    weight_grad = pl.pallas_call(
        order_kernel,
        name="order",
        grid=(head_size // chunk,),
        in_specs=[pl.BlockSpec((RING, chunk, quarter, column_block), lambda i: (0, i, 0, 0))],
        out_specs=pl.BlockSpec((chunk, RING, quarter, column_block), lambda i: (i, 0, 0, 0)),
        out_shape=jax.ShapeDtypeStruct((head_size, RING, quarter, column_block), bf16),
        cost_estimate=cost(10**5, 4 * 10**6),
    )(all_quarters).reshape(head_size * columns_here, column_block)
    return (input_grad, gate_grad, weight_grad)


def solution(mesh):
    in_specs = (
        P("seq", None),
        P(None, "head"),
        P("seq", "head"),
        P("seq", "head"),
        P("seq", "head"),
        P("seq", "head"),
        P("seq", None, None),
        P("seq", None, None),
        P("head"),
    )
    out_specs = (P("seq", "head"), P("seq", "head"), P(None, "head"))
    return jax.shard_map(
        on_device, mesh=mesh, in_specs=in_specs, out_specs=out_specs, check_vma=False
    )
```

```python
import functools
import math

import jax
import jax.numpy as jnp
from jax import lax
from jax.experimental import pallas as pl
from jax.experimental.pallas import tpu as pltpu
from jax.sharding import PartitionSpec as P

HEAD_COUNT = 128
G = 4
RING = 4
EXTRA = 16

f32 = jnp.float32
bf16 = jnp.bfloat16
VMEM = pl.BlockSpec(memory_space=pltpu.VMEM)
SMEM = pl.BlockSpec(memory_space=pltpu.SMEM)
NT = (((1,), (1,)), ((), ()))
TN = (((0,), (0,)), ((), ()))


def by_head(columns, width):
    rows, heads = columns.shape
    head = lax.broadcasted_iota(jnp.int32, (rows, heads * width), 1) // width
    out = jnp.broadcast_to(columns[:, :1], (rows, heads * width))
    for h in range(1, heads):
        out = jnp.where(head == h, columns[:, h : h + 1], out)
    return out


def part_kernel(scale, x_ref, gate, saved, grad, *rest):
    outs, turned, ordered = rest[:RING], rest[RING], rest[RING + 1]
    blocks, rows, columns = outs[0].shape

    @pl.when(pl.program_id(0) == 0)
    def _():
        value = gate[...].astype(f32)
        gated = saved[...].astype(f32) * (value * jax.nn.sigmoid(value))
        turned[...] = gated.T
        for j in range(RING):
            start = pl.multiple_of((x_ref[0] + j) % RING * rows, rows)
            ordered[j * rows : (j + 1) * rows] = turned[pl.ds(start, rows)].astype(bf16)

    product = jnp.dot(ordered[...], grad[...], preferred_element_type=f32) * scale
    for b in range(blocks):
        piece = product[:, b * columns : (b + 1) * columns].astype(bf16)
        for j in range(RING):
            outs[j][b] = piece[j * rows : (j + 1) * rows]


def ring_sum_kernel(starts, *refs):
    terms, out = refs[:-1], refs[-1]
    window = out.shape[1]
    for k, start in enumerate(starts):
        rows = slice(start, start + window)
        out[k] = sum(t[rows].astype(f32) for t in terms).astype(bf16)


def line_sum_kernel(windows, out):
    total = sum(windows[k].astype(f32) for k in range(windows.shape[0])).astype(bf16)
    for k in range(out.shape[0]):
        out[k] = total


def assemble_kernel(starts, windows, out):
    ends = starts[1:] + [out.shape[0]]
    for k, (start, end) in enumerate(zip(starts, ends)):
        out[start:end] = windows[k, : end - start]


def write_log(message, h, total):
    rows = message.shape[2] - EXTRA
    high = total.astype(bf16).astype(f32)
    middle = (total - high).astype(bf16).astype(f32)
    low = total - high - middle
    place = lax.broadcasted_iota(jnp.int32, (EXTRA, total.shape[1]), 0)
    tail = jnp.where(
        place == 0, high, jnp.where(place == 1, middle, jnp.where(place == 2, low, 0.0))
    )
    for k in range(message.shape[0]):
        message[k, h, rows:] = tail.astype(bf16)


def read_log(message, k, h):
    rows = message.shape[2] - EXTRA
    tail = message[k, h, rows:].astype(f32)
    return tail[0:1] + tail[1:2] + tail[2:3]


def upstream_kernel(x_ref, grad, *refs):
    panels = refs[:RING]
    gate, saved, cumulative, out_group, gate_grad, scan_grad, message, total = refs[RING:]
    step = pl.program_id(0)
    blocks, rows, columns = panels[0].shape
    weights = jnp.concatenate(
        [jnp.concatenate([p[b] for p in panels], axis=0) for b in range(blocks)], axis=1
    )
    product = lax.dot_general(grad[...], weights, NT, preferred_element_type=f32)

    @pl.when(step == 0)
    def _():
        total[...] = product

    @pl.when(step > 0)
    def _():
        total[...] += product

    @pl.when(step == pl.num_programs(0) - 1)
    def _():
        upstream = pltpu.roll(total[...], x_ref[0] * rows, 1)
        value = gate[...].astype(f32)
        sig = jax.nn.sigmoid(value)
        gate_grad[...] = (
            upstream * saved[...].astype(f32) * sig * (1.0 + value * (1.0 - sig))
        ).astype(bf16)
        scan = (upstream * (value * sig)).astype(bf16)
        scan_grad[...] = scan
        heads = cumulative.shape[1]
        width = scan.shape[1] // heads
        weighted = scan.astype(f32) * by_head(jnp.exp(cumulative[...]), width)
        local = lax.dot_general(
            weighted.astype(bf16), out_group[...], TN, preferred_element_type=f32
        )
        states = local.shape[1]
        for h in range(heads):
            term = local[h * width : (h + 1) * width].astype(bf16)
            for k in range(message.shape[0]):
                message[k, h, :width] = term
            last = jnp.broadcast_to(cumulative[cumulative.shape[0] - 1 :, h : h + 1], (1, states))
            write_log(message, h, last)


def row_kernel(x_ref, *refs):
    received, (message, in_row, tail_log) = refs[:RING], refs[RING:]
    x = x_ref[0]
    _, heads, rows, states = message.shape
    width = rows - EXTRA
    for h in range(heads):
        carry = jnp.zeros((width, states), f32)
        logs = jnp.zeros((1, states), f32)

        def further(j, keep, carry, logs):
            log = read_log(received[j], 0, h)
            term = received[j][0, h, :width].astype(f32) + jnp.exp(log) * carry
            return jnp.where(keep, term, carry), jnp.where(keep, logs + log, logs)

        for j in reversed(range(1, RING)):
            carry, logs = further(j, x + j < RING, carry, logs)
        in_row[h] = carry
        tail_log[h] = jnp.broadcast_to(logs, tail_log.shape[1:])
        carry, logs = further(0, x >= 0, carry, logs)
        for j in reversed(range(1, RING)):
            carry, logs = further(j, x + j >= RING, carry, logs)
        message[0, h, :width] = carry.astype(bf16)
        write_log(message, h, logs)


def inside_kernel(in_group, out_group, cumulative, turned, scan_grad, step_size, skip_gain, out):
    length, heads = cumulative.shape
    width = scan_grad.shape[1] // heads
    size = 128
    for start in range(0, length, size):
        here = slice(start, start + size)
        dots = lax.dot_general(
            in_group[here], out_group[start:], NT, preferred_element_type=f32
        )
        t = lax.broadcasted_iota(jnp.int32, dots.shape, 0)
        s = lax.broadcasted_iota(jnp.int32, dots.shape, 1)
        terms = []
        for h in range(heads):
            spread = turned[h : h + 1, start:] - cumulative[here, h : h + 1]
            factor = jnp.where(t <= s, jnp.exp(jnp.minimum(spread, 0.0)), 0.0)
            terms.append(
                jnp.dot(
                    (dots * factor).astype(bf16),
                    scan_grad[start:, h * width : (h + 1) * width],
                    preferred_element_type=f32,
                )
            )
        inside = jnp.concatenate(terms, axis=1)
        out[here] = by_head(step_size[here], width) * inside + by_head(
            jnp.broadcast_to(skip_gain[...], (size, heads)), width
        ) * scan_grad[here].astype(f32)


def carried_kernel(rows_z, z_ref, *refs):
    received = refs[: rows_z - 1]
    in_row, tail_log, in_group, cumulative, step_size, partial, out = refs[rows_z - 1 :]
    z = z_ref[0]
    _, heads, rows, states = received[0].shape
    width = rows - EXTRA
    length = cumulative.shape[0]
    terms = []
    for h in range(heads):
        carry = jnp.zeros((width, states), f32)
        for j in reversed(range(1, rows_z)):
            message = received[j - 1]
            term = message[0, h, :width].astype(f32)
            term = term + jnp.exp(read_log(message, 0, h)) * carry
            carry = jnp.where(z + j < rows_z, term, carry)
        carried = in_row[h] + jnp.exp(tail_log[h, 0:1]) * carry
        terms.append(
            lax.dot_general(in_group[...], carried.astype(bf16), NT, preferred_element_type=f32)
        )
    decay = jnp.exp(cumulative[length - 1 :] - cumulative[...])
    scale = by_head(step_size[...] * decay, width)
    out[...] = (partial[...] + scale * jnp.concatenate(terms, axis=1)).astype(bf16)


def cost(flops, bytes_accessed, transcendentals=0):
    return pl.CostEstimate(
        flops=flops, bytes_accessed=bytes_accessed, transcendentals=transcendentals
    )


def along_x(block, step):
    rows = lax.axis_size("seq")
    route = [(i, i // RING * RING + (i + step) % RING) for i in range(rows)]
    return lax.ppermute(block, "seq", route)


def to_group(blocks, groups):
    return lax.all_to_all(
        blocks, "seq", split_axis=0, concat_axis=0, tiled=True, axis_index_groups=groups
    )


def after(value, *others):
    return lax.optimization_barrier((value, *others))[0]


def on_device(
    out_grad,
    out_weight,
    gate_input,
    scan_output,
    step_size,
    log_decay,
    input_map,
    output_map,
    skip_gain,
):
    length, width = out_grad.shape
    heads_here = log_decay.shape[1]
    columns_here = gate_input.shape[1]
    head_width = columns_here // heads_here
    seq_size = lax.axis_size("seq")
    head_size = lax.axis_size("head")
    rows_z = seq_size // RING
    quarter = columns_here // RING
    column_block = width // head_size
    states = input_map.shape[2]
    message_rows = head_width + EXTRA
    me = lax.axis_index("seq")
    x = (me % RING).astype(jnp.int32)
    z = (me // RING).astype(jnp.int32)
    rings = [[r * RING + i for i in range(RING)] for r in range(rows_z)]
    lines = [[r * RING + i for r in range(rows_z)] for i in range(RING)]
    steps = 2
    blocks = head_size // steps
    wide = blocks * column_block

    weight_quarter = lax.dynamic_index_in_dim(
        out_weight.reshape(head_size, RING, quarter, column_block),
        x,
        1,
        keepdims=False,
    )
    rows_quarter = lax.all_to_all(weight_quarter, "head", split_axis=0, concat_axis=0, tiled=True)

    group_index = lax.axis_index("head") * heads_here // (HEAD_COUNT // G)
    in_group = lax.dynamic_index_in_dim(input_map, group_index, 1, keepdims=False)
    out_group = lax.dynamic_index_in_dim(output_map, group_index, 1, keepdims=False)
    cumulative = jnp.cumsum(log_decay, axis=0)
    turned = cumulative.T

    half = head_size // 2
    whole = lambda shape: pl.BlockSpec(shape, lambda *_: (0,) * len(shape))
    block_shape = (half, quarter, column_block)
    quarter_shape = (head_size, quarter, column_block)
    x_place = x.reshape(1)
    own, forth, opposite, back = pl.pallas_call(
        functools.partial(part_kernel, 1.0 / math.sqrt(length * seq_size)),
        name="block_parts",
        grid=(2,),
        in_specs=[
            SMEM,
            whole((length, columns_here)),
            whole((length, columns_here)),
            pl.BlockSpec((length, half * column_block), lambda i: (0, i)),
        ],
        out_specs=[pl.BlockSpec(block_shape, lambda i: (i, 0, 0))] * RING,
        out_shape=[jax.ShapeDtypeStruct(quarter_shape, bf16)] * RING,
        scratch_shapes=[
            pltpu.VMEM((columns_here, length), f32),
            pltpu.VMEM((columns_here, length), bf16),
        ],
        cost_estimate=cost(2 * length * width * columns_here, 2 * length * width),
    )(x_place, gate_input, scan_output, out_grad)
    own, rows_quarter, in_group, out_group, cumulative, turned, step_size = lax.optimization_barrier(
        (own, rows_quarter, in_group, out_group, cumulative, turned, step_size)
    )
    window = -(-head_size // rows_z)
    starts = [k * (head_size - window) // (rows_z - 1) for k in range(rows_z)]
    windows_shape = jax.ShapeDtypeStruct((rows_z, window, quarter, column_block), bf16)
    windows = pl.pallas_call(
        functools.partial(ring_sum_kernel, starts),
        name="ring_sum",
        in_specs=[VMEM] * RING,
        out_specs=VMEM,
        out_shape=windows_shape,
        cost_estimate=cost(10**6, 4 * 10**6),
    )(own, along_x(opposite, 2), along_x(forth, 1), along_x(back, -1))
    windows, rows_quarter = lax.optimization_barrier((windows, rows_quarter))
    panels = [
        rows_quarter,
        along_x(rows_quarter, -1),
        along_x(rows_quarter, 2),
        along_x(rows_quarter, 1),
    ]
    from_line = to_group(windows, lines)
    reduced = pl.pallas_call(
        line_sum_kernel,
        name="line_sum",
        in_specs=[VMEM],
        out_specs=VMEM,
        out_shape=windows_shape,
        cost_estimate=cost(10**6, 2 * 10**6),
    )(from_line)
    gathered = to_group(reduced, lines)
    panels, gathered = lax.optimization_barrier((panels, gathered))


    panel_shape = (length, columns_here)
    gate_grad, scan_grad, message = pl.pallas_call(
        upstream_kernel,
        name="upstream",
        grid=(steps,),
        in_specs=[
            SMEM,
            pl.BlockSpec((length, wide), lambda i: (0, i)),
            *[pl.BlockSpec((blocks, quarter, column_block), lambda i: (i, 0, 0))] * RING,
            whole(panel_shape),
            whole(panel_shape),
            whole((length, heads_here)),
            whole((length, states)),
        ],
        out_specs=[
            whole(panel_shape),
            whole(panel_shape),
            whole((1, heads_here, message_rows, states)),
        ],
        out_shape=[
            jax.ShapeDtypeStruct(panel_shape, bf16),
            jax.ShapeDtypeStruct(panel_shape, bf16),
            jax.ShapeDtypeStruct((1, heads_here, message_rows, states), bf16),
        ],
        scratch_shapes=[pltpu.VMEM(panel_shape, f32)],
        cost_estimate=cost(2 * length * width * columns_here, 2 * length * width),
    )(x_place, out_grad, *panels, gate_input, scan_output, cumulative, out_group)

    state = (heads_here, head_width, states)
    partial = pl.pallas_call(
        inside_kernel,
        name="inside",
        in_specs=[VMEM] * 7,
        out_specs=VMEM,
        out_shape=jax.ShapeDtypeStruct(panel_shape, f32),
        cost_estimate=cost(4 * 10**8, 2 * 10**6, 2 * length * length),
    )(
        in_group,
        out_group,
        cumulative,
        turned,
        scan_grad,
        step_size,
        skip_gain.reshape(1, heads_here),
    )
    on_ring = [message if j == 0 else along_x(message, -j) for j in range(RING)]
    row_message, in_row, tail_log = pl.pallas_call(
        row_kernel,
        name="row_scan",
        in_specs=[SMEM] + [VMEM] * RING,
        out_specs=[VMEM, VMEM, VMEM],
        out_shape=[
            jax.ShapeDtypeStruct((1, heads_here, message_rows, states), bf16),
            jax.ShapeDtypeStruct(state, f32),
            jax.ShapeDtypeStruct((heads_here, 8, states), f32),
        ],
        cost_estimate=cost(10**6, 10**6),
    )(x_place, *on_ring)
    from_rows = [
        lax.ppermute(
            row_message, "seq", [(i + j * RING, i) for i in range(seq_size - j * RING)]
        )
        for j in range(1, rows_z)
    ]
    input_grad = pl.pallas_call(
        functools.partial(carried_kernel, rows_z),
        name="carried",
        in_specs=[SMEM] + [VMEM] * (5 + rows_z),
        out_specs=VMEM,
        out_shape=jax.ShapeDtypeStruct(panel_shape, bf16),
        cost_estimate=cost(10**8, 10**6),
    )(z.reshape(1), *from_rows, in_row, tail_log, in_group, cumulative, step_size, partial)

    quarter_sum = pl.pallas_call(
        functools.partial(assemble_kernel, starts),
        name="assemble",
        in_specs=[VMEM],
        out_specs=VMEM,
        out_shape=jax.ShapeDtypeStruct(quarter_shape, bf16),
        cost_estimate=cost(10**5, 10**6),
    )(gathered)
    pieces = lax.all_to_all(quarter_sum, "head", split_axis=0, concat_axis=0, tiled=True)
    pieces = after(pieces, row_message, partial)
    quarters = [pieces, along_x(pieces, -1), along_x(pieces, 2), along_x(pieces, 1)]
    weight_grad = jnp.zeros((head_size, RING, quarter, column_block), bf16)
    for j in (0, 1, 3, 2):
        weight_grad = lax.dynamic_update_slice_in_dim(
            weight_grad, quarters[j][:, None], (x + j) % RING, 1
        )
    weight_grad = weight_grad.reshape(head_size * columns_here, column_block)
    return (input_grad, gate_grad, weight_grad)


def solution(mesh):
    in_specs = (
        P("seq", None),
        P(None, "head"),
        P("seq", "head"),
        P("seq", "head"),
        P("seq", "head"),
        P("seq", "head"),
        P("seq", None, None),
        P("seq", None, None),
        P("head"),
    )
    out_specs = (P("seq", "head"), P("seq", "head"), P(None, "head"))
    return jax.shard_map(
        on_device, mesh=mesh, in_specs=in_specs, out_specs=out_specs, check_vma=False
    )
```

```python
import functools
import math

import jax
import jax.numpy as jnp
from jax import lax
from jax.experimental import pallas as pl
from jax.experimental.pallas import tpu as pltpu
from jax.sharding import PartitionSpec as P

HEAD_COUNT = 128
G = 4
RING = 4
EXTRA = 16

f32 = jnp.float32
bf16 = jnp.bfloat16
VMEM = pl.BlockSpec(memory_space=pltpu.VMEM)
SMEM = pl.BlockSpec(memory_space=pltpu.SMEM)
NT = (((1,), (1,)), ((), ()))
TN = (((0,), (0,)), ((), ()))


def by_head(columns, width):
    rows, heads = columns.shape
    head = lax.broadcasted_iota(jnp.int32, (rows, heads * width), 1) // width
    out = jnp.broadcast_to(columns[:, :1], (rows, heads * width))
    for h in range(1, heads):
        out = jnp.where(head == h, columns[:, h : h + 1], out)
    return out


def part_kernel(scale, x_ref, gate, saved, grad, *rest):
    outs, turned, ordered = rest[:RING], rest[RING], rest[RING + 1]
    blocks, rows, columns = outs[0].shape

    @pl.when(pl.program_id(0) == 0)
    def _():
        value = gate[...].astype(f32)
        gated = saved[...].astype(f32) * (value * jax.nn.sigmoid(value))
        turned[...] = gated.T
        for j in range(RING):
            start = pl.multiple_of((x_ref[0] + j) % RING * rows, rows)
            ordered[j * rows : (j + 1) * rows] = turned[pl.ds(start, rows)].astype(bf16)

    product = jnp.dot(ordered[...], grad[...], preferred_element_type=f32) * scale
    for b in range(blocks):
        piece = product[:, b * columns : (b + 1) * columns].astype(bf16)
        for j in range(RING):
            outs[j][b] = piece[j * rows : (j + 1) * rows]


def window_starts(rows_z, half):
    window = -(-half // rows_z)
    return window, [k * (half - window) // (rows_z - 1) for k in range(rows_z)]


def window_of(rows_z, half, k):
    starts = window_starts(rows_z, half)[1]
    k = k % rows_z
    start = jnp.int32(starts[0])
    for i in range(1, rows_z):
        start = jnp.where(k == i, starts[i], start)
    return start


def ring_sum_kernel(rows_z, z_ref, *refs):
    terms, outs = refs[:RING], refs[RING:]
    half, window = terms[0].shape[0] // 2, outs[0].shape[0]
    for which in range(2):
        for j in range(rows_z):
            rows = pl.ds(window_of(rows_z, half, z_ref[0] + j) + which * half, window)
            outs[which * rows_z + j][...] = sum(t[rows].astype(f32) for t in terms).astype(bf16)


def assemble_kernel(rows_z, z_ref, *refs):
    pieces, out = refs[:-1], refs[-1]
    half = out.shape[0] // 2
    window = pieces[0].shape[0]
    for which in range(2):
        for j in range(rows_z):
            start = window_of(rows_z, half, z_ref[0] + j) + which * half
            out[pl.ds(start, window)] = pieces[which * rows_z + j][...]


def write_log(message, h, total):
    rows = message.shape[2] - EXTRA
    high = total.astype(bf16).astype(f32)
    middle = (total - high).astype(bf16).astype(f32)
    low = total - high - middle
    place = lax.broadcasted_iota(jnp.int32, (EXTRA, total.shape[1]), 0)
    tail = jnp.where(
        place == 0, high, jnp.where(place == 1, middle, jnp.where(place == 2, low, 0.0))
    )
    for k in range(message.shape[0]):
        message[k, h, rows:] = tail.astype(bf16)


def read_log(message, k, h):
    rows = message.shape[2] - EXTRA
    tail = message[k, h, rows:].astype(f32)
    return tail[0:1] + tail[1:2] + tail[2:3]


def upstream_kernel(
    grad, panel, gate, saved, cumulative, out_group, gate_grad, scan_grad, message, total
):
    step = pl.program_id(0)
    quarters, blocks, rows, columns = panel.shape
    weights = jnp.concatenate(
        [panel[:, b].reshape(quarters * rows, columns) for b in range(blocks)], axis=1
    )
    product = lax.dot_general(grad[...], weights, NT, preferred_element_type=f32)

    @pl.when(step == 0)
    def _():
        total[...] = product

    @pl.when(step > 0)
    def _():
        total[...] += product

    @pl.when(step == pl.num_programs(0) - 1)
    def _():
        upstream = total[...]
        value = gate[...].astype(f32)
        sig = jax.nn.sigmoid(value)
        gate_grad[...] = (
            upstream * saved[...].astype(f32) * sig * (1.0 + value * (1.0 - sig))
        ).astype(bf16)
        scan = (upstream * (value * sig)).astype(bf16)
        scan_grad[...] = scan
        heads = cumulative.shape[1]
        width = scan.shape[1] // heads
        weighted = scan.astype(f32) * by_head(jnp.exp(cumulative[...]), width)
        local = lax.dot_general(
            weighted.astype(bf16), out_group[...], TN, preferred_element_type=f32
        )
        states = local.shape[1]
        for h in range(heads):
            term = local[h * width : (h + 1) * width].astype(bf16)
            for k in range(message.shape[0]):
                message[k, h, :width] = term
            last = jnp.broadcast_to(cumulative[cumulative.shape[0] - 1 :, h : h + 1], (1, states))
            write_log(message, h, last)


def row_kernel(x_ref, *refs):
    received, (message, in_row, tail_log) = refs[:RING], refs[RING:]
    x = x_ref[0]
    _, heads, rows, states = message.shape
    width = rows - EXTRA
    for h in range(heads):
        carry = jnp.zeros((width, states), f32)
        logs = jnp.zeros((1, states), f32)

        def further(j, keep, carry, logs):
            log = read_log(received[j], 0, h)
            term = received[j][0, h, :width].astype(f32) + jnp.exp(log) * carry
            return jnp.where(keep, term, carry), jnp.where(keep, logs + log, logs)

        for j in reversed(range(1, RING)):
            carry, logs = further(j, x + j < RING, carry, logs)
        in_row[h] = carry
        tail_log[h] = jnp.broadcast_to(logs, tail_log.shape[1:])
        carry, logs = further(0, x >= 0, carry, logs)
        for j in reversed(range(1, RING)):
            carry, logs = further(j, x + j >= RING, carry, logs)
        message[0, h, :width] = carry.astype(bf16)
        write_log(message, h, logs)


def inside_kernel(in_group, out_group, cumulative, turned, scan_grad, step_size, skip_gain, out):
    length, heads = cumulative.shape
    width = scan_grad.shape[1] // heads
    size = 128
    for start in range(0, length, size):
        here = slice(start, start + size)
        dots = lax.dot_general(
            in_group[here], out_group[start:], NT, preferred_element_type=f32
        )
        t = lax.broadcasted_iota(jnp.int32, dots.shape, 0)
        s = lax.broadcasted_iota(jnp.int32, dots.shape, 1)
        terms = []
        for h in range(heads):
            spread = turned[h : h + 1, start:] - cumulative[here, h : h + 1]
            factor = jnp.where(t <= s, jnp.exp(jnp.minimum(spread, 0.0)), 0.0)
            terms.append(
                jnp.dot(
                    (dots * factor).astype(bf16),
                    scan_grad[start:, h * width : (h + 1) * width],
                    preferred_element_type=f32,
                )
            )
        inside = jnp.concatenate(terms, axis=1)
        out[here] = by_head(step_size[here], width) * inside + by_head(
            jnp.broadcast_to(skip_gain[...], (size, heads)), width
        ) * scan_grad[here].astype(f32)


def carried_kernel(rows_z, z_ref, *refs):
    received = refs[: rows_z - 1]
    in_row, tail_log, in_group, cumulative, step_size, partial, out = refs[rows_z - 1 :]
    z = z_ref[0]
    _, heads, rows, states = received[0].shape
    width = rows - EXTRA
    length = cumulative.shape[0]
    terms = []
    for h in range(heads):
        carry = jnp.zeros((width, states), f32)
        for j in reversed(range(1, rows_z)):
            message = received[j - 1]
            term = message[0, h, :width].astype(f32)
            term = term + jnp.exp(read_log(message, 0, h)) * carry
            carry = jnp.where(z + j < rows_z, term, carry)
        carried = in_row[h] + jnp.exp(tail_log[h, 0:1]) * carry
        terms.append(
            lax.dot_general(in_group[...], carried.astype(bf16), NT, preferred_element_type=f32)
        )
    decay = jnp.exp(cumulative[length - 1 :] - cumulative[...])
    scale = by_head(step_size[...] * decay, width)
    out[...] = (partial[...] + scale * jnp.concatenate(terms, axis=1)).astype(bf16)


def cost(flops, bytes_accessed, transcendentals=0):
    return pl.CostEstimate(
        flops=flops, bytes_accessed=bytes_accessed, transcendentals=transcendentals
    )


def along_x(block, step):
    rows = lax.axis_size("seq")
    route = [(i, i // RING * RING + (i + step) % RING) for i in range(rows)]
    return lax.ppermute(block, "seq", route)


def along_z(block, step):
    size = lax.axis_size("seq")
    return lax.ppermute(block, "seq", [(i, (i + RING * step) % size) for i in range(size)])


def total_of(*terms):
    return sum(t.astype(f32) for t in terms).astype(bf16)


def to_group(blocks, groups):
    return lax.all_to_all(
        blocks, "seq", split_axis=0, concat_axis=0, tiled=True, axis_index_groups=groups
    )


def after(value, *others):
    return lax.optimization_barrier((value, *others))[0]


def on_device(
    out_grad,
    out_weight,
    gate_input,
    scan_output,
    step_size,
    log_decay,
    input_map,
    output_map,
    skip_gain,
):
    length, width = out_grad.shape
    heads_here = log_decay.shape[1]
    columns_here = gate_input.shape[1]
    head_width = columns_here // heads_here
    seq_size = lax.axis_size("seq")
    head_size = lax.axis_size("head")
    rows_z = seq_size // RING
    quarter = columns_here // RING
    column_block = width // head_size
    states = input_map.shape[2]
    message_rows = head_width + EXTRA
    me = lax.axis_index("seq")
    x = (me % RING).astype(jnp.int32)
    z = (me // RING).astype(jnp.int32)
    rings = [[r * RING + i for i in range(RING)] for r in range(rows_z)]
    steps = 2
    blocks = head_size // steps
    wide = blocks * column_block

    half = head_size // 2
    whole = lambda shape: pl.BlockSpec(shape, lambda *_: (0,) * len(shape))
    block_shape = (half, quarter, column_block)
    quarter_shape = (head_size, quarter, column_block)
    x_place = x.reshape(1)
    own, forth, opposite, back = pl.pallas_call(
        functools.partial(part_kernel, 1.0 / math.sqrt(length * seq_size)),
        name="block_parts",
        grid=(2,),
        in_specs=[
            SMEM,
            whole((length, columns_here)),
            whole((length, columns_here)),
            pl.BlockSpec((length, half * column_block), lambda i: (0, i)),
        ],
        out_specs=[pl.BlockSpec(block_shape, lambda i: (i, 0, 0))] * RING,
        out_shape=[jax.ShapeDtypeStruct(quarter_shape, bf16)] * RING,
        scratch_shapes=[
            pltpu.VMEM((columns_here, length), f32),
            pltpu.VMEM((columns_here, length), bf16),
        ],
        cost_estimate=cost(2 * length * width * columns_here, 2 * length * width),
    )(x_place, gate_input, scan_output, out_grad)
    window = window_starts(rows_z, half)[0]
    z_place = z.reshape(1)
    windows = pl.pallas_call(
        functools.partial(ring_sum_kernel, rows_z),
        name="ring_sum",
        in_specs=[SMEM] + [VMEM] * RING,
        out_specs=[VMEM] * (2 * rows_z),
        out_shape=[jax.ShapeDtypeStruct((window, quarter, column_block), bf16)] * (2 * rows_z),
        cost_estimate=cost(10**6, 4 * 10**6),
    )(z_place, own, along_x(opposite, 2), along_x(forth, 1), along_x(back, -1))
    windows_a, windows_b = windows[:rows_z], windows[rows_z:]
    reduced = [
        total_of(w[0], *(along_z(w[j], j) for j in range(1, rows_z)))
        for w in (windows_a, windows_b)
    ]
    gathered = [r if j == 0 else along_z(r, -j) for r in reduced for j in range(rows_z)]

    group_index = lax.axis_index("head") * heads_here // (HEAD_COUNT // G)
    in_group = lax.dynamic_index_in_dim(input_map, group_index, 1, keepdims=False)
    out_group = lax.dynamic_index_in_dim(output_map, group_index, 1, keepdims=False)
    cumulative = jnp.cumsum(log_decay, axis=0)
    turned = cumulative.T

    weight_quarter = lax.dynamic_index_in_dim(
        out_weight.reshape(head_size, RING, quarter, column_block),
        x,
        1,
        keepdims=False,
    )
    rows_quarter = lax.all_to_all(weight_quarter, "head", split_axis=0, concat_axis=0, tiled=True)
    rows_quarter, in_group, out_group, cumulative, turned, step_size, _, _ = lax.optimization_barrier(
        (
            rows_quarter,
            in_group,
            out_group,
            cumulative,
            turned,
            step_size,
            windows_a[0],
            windows_b[0],
        )
    )
    panel = to_group(jnp.broadcast_to(rows_quarter[None], (RING, *rows_quarter.shape)), rings)
    panel = after(panel, *reduced)

    panel_shape = (length, columns_here)
    gate_grad, scan_grad, message = pl.pallas_call(
        upstream_kernel,
        name="upstream",
        grid=(steps,),
        in_specs=[
            pl.BlockSpec((length, wide), lambda i: (0, i)),
            pl.BlockSpec((RING, blocks, quarter, column_block), lambda i: (0, i, 0, 0)),
            whole(panel_shape),
            whole(panel_shape),
            whole((length, heads_here)),
            whole((length, states)),
        ],
        out_specs=[
            whole(panel_shape),
            whole(panel_shape),
            whole((1, heads_here, message_rows, states)),
        ],
        out_shape=[
            jax.ShapeDtypeStruct(panel_shape, bf16),
            jax.ShapeDtypeStruct(panel_shape, bf16),
            jax.ShapeDtypeStruct((1, heads_here, message_rows, states), bf16),
        ],
        scratch_shapes=[pltpu.VMEM(panel_shape, f32)],
        cost_estimate=cost(2 * length * width * columns_here, 2 * length * width),
    )(out_grad, panel, gate_input, scan_output, cumulative, out_group)

    state = (heads_here, head_width, states)
    partial = pl.pallas_call(
        inside_kernel,
        name="inside",
        in_specs=[VMEM] * 7,
        out_specs=VMEM,
        out_shape=jax.ShapeDtypeStruct(panel_shape, f32),
        cost_estimate=cost(4 * 10**8, 2 * 10**6, 2 * length * length),
    )(
        in_group,
        out_group,
        cumulative,
        turned,
        scan_grad,
        step_size,
        skip_gain.reshape(1, heads_here),
    )
    on_ring = [message if j == 0 else along_x(message, -j) for j in range(RING)]
    row_message, in_row, tail_log = pl.pallas_call(
        row_kernel,
        name="row_scan",
        in_specs=[SMEM] + [VMEM] * RING,
        out_specs=[VMEM, VMEM, VMEM],
        out_shape=[
            jax.ShapeDtypeStruct((1, heads_here, message_rows, states), bf16),
            jax.ShapeDtypeStruct(state, f32),
            jax.ShapeDtypeStruct((heads_here, 8, states), f32),
        ],
        cost_estimate=cost(10**6, 10**6),
    )(x_place, *on_ring)
    from_rows = [
        lax.ppermute(
            row_message, "seq", [(i + j * RING, i) for i in range(seq_size - j * RING)]
        )
        for j in range(1, rows_z)
    ]
    quarter_sum = pl.pallas_call(
        functools.partial(assemble_kernel, rows_z),
        name="assemble",
        in_specs=[SMEM] + [VMEM] * (2 * rows_z),
        out_specs=VMEM,
        out_shape=jax.ShapeDtypeStruct((head_size, quarter, column_block), bf16),
        cost_estimate=cost(10**5, 10**6),
    )(z_place, *gathered)
    pieces = lax.all_to_all(quarter_sum, "head", split_axis=0, concat_axis=0, tiled=True)
    pieces = after(pieces, row_message, partial)
    quarters = [pieces, along_x(pieces, -1), along_x(pieces, 2), along_x(pieces, 1)]
    partial = after(partial, *quarters)
    weight_grad = jnp.zeros((head_size, RING, quarter, column_block), bf16)
    for j in (0, 1, 3, 2):
        weight_grad = lax.dynamic_update_slice_in_dim(
            weight_grad, quarters[j][:, None], (x + j) % RING, 1
        )
    weight_grad = weight_grad.reshape(head_size * columns_here, column_block)

    input_grad = pl.pallas_call(
        functools.partial(carried_kernel, rows_z),
        name="carried",
        in_specs=[SMEM] + [VMEM] * (5 + rows_z),
        out_specs=VMEM,
        out_shape=jax.ShapeDtypeStruct(panel_shape, bf16),
        cost_estimate=cost(10**8, 10**6),
    )(z.reshape(1), *from_rows, in_row, tail_log, in_group, cumulative, step_size, partial)

    return (input_grad, gate_grad, weight_grad)


def solution(mesh):
    in_specs = (
        P("seq", None),
        P(None, "head"),
        P("seq", "head"),
        P("seq", "head"),
        P("seq", "head"),
        P("seq", "head"),
        P("seq", None, None),
        P("seq", None, None),
        P("head"),
    )
    out_specs = (P("seq", "head"), P("seq", "head"), P(None, "head"))
    return jax.shard_map(
        on_device, mesh=mesh, in_specs=in_specs, out_specs=out_specs, check_vma=False
    )
```

```python
import functools
import math

import jax
import jax.numpy as jnp
from jax import lax
from jax.experimental import pallas as pl
from jax.experimental.pallas import tpu as pltpu
from jax.sharding import PartitionSpec as P

HEAD_COUNT = 128
G = 4
RING = 4
EXTRA = 16

f32 = jnp.float32
bf16 = jnp.bfloat16
VMEM = pl.BlockSpec(memory_space=pltpu.VMEM)
SMEM = pl.BlockSpec(memory_space=pltpu.SMEM)
NT = (((1,), (1,)), ((), ()))
TN = (((0,), (0,)), ((), ()))


def by_head(columns, width):
    rows, heads = columns.shape
    head = lax.broadcasted_iota(jnp.int32, (rows, heads * width), 1) // width
    out = jnp.broadcast_to(columns[:, :1], (rows, heads * width))
    for h in range(1, heads):
        out = jnp.where(head == h, columns[:, h : h + 1], out)
    return out


def part_kernel(scale, x_ref, gate, saved, grad, *rest):
    outs, turned, ordered = rest[:RING], rest[RING], rest[RING + 1]
    blocks, rows, columns = outs[0].shape

    @pl.when(pl.program_id(0) == 0)
    def _():
        value = gate[...].astype(f32)
        gated = saved[...].astype(f32) * (value * jax.nn.sigmoid(value))
        turned[...] = gated.T
        for j in range(RING):
            start = pl.multiple_of((x_ref[0] + j) % RING * rows, rows)
            ordered[j * rows : (j + 1) * rows] = turned[pl.ds(start, rows)].astype(bf16)

    product = jnp.dot(ordered[...], grad[...], preferred_element_type=f32) * scale
    for b in range(blocks):
        piece = product[:, b * columns : (b + 1) * columns].astype(bf16)
        for j in range(RING):
            outs[j][b] = piece[j * rows : (j + 1) * rows]


def window_starts(rows_z, half):
    window = -(-half // rows_z)
    return window, [k * (half - window) // (rows_z - 1) for k in range(rows_z)]


def window_of(rows_z, half, k):
    starts = window_starts(rows_z, half)[1]
    k = k % rows_z
    start = jnp.int32(starts[0])
    for i in range(1, rows_z):
        start = jnp.where(k == i, starts[i], start)
    return start


def ring_sum_kernel(rows_z, z_ref, *refs):
    terms, outs = refs[:RING], refs[RING:]
    half, window = terms[0].shape[0] // 2, outs[0].shape[0]
    for which in range(2):
        for j in range(rows_z):
            rows = pl.ds(window_of(rows_z, half, z_ref[0] + j) + which * half, window)
            outs[which * rows_z + j][...] = sum(t[rows].astype(f32) for t in terms).astype(bf16)


def assemble_kernel(rows_z, z_ref, *refs):
    pieces, out = refs[:-1], refs[-1]
    half = out.shape[0] // 2
    window = pieces[0].shape[0]
    for which in range(2):
        for j in range(rows_z):
            start = window_of(rows_z, half, z_ref[0] + j) + which * half
            out[pl.ds(start, window)] = pieces[which * rows_z + j][...]


def write_log(message, h, total):
    rows = message.shape[2] - EXTRA
    high = total.astype(bf16).astype(f32)
    middle = (total - high).astype(bf16).astype(f32)
    low = total - high - middle
    place = lax.broadcasted_iota(jnp.int32, (EXTRA, total.shape[1]), 0)
    tail = jnp.where(
        place == 0, high, jnp.where(place == 1, middle, jnp.where(place == 2, low, 0.0))
    )
    for k in range(message.shape[0]):
        message[k, h, rows:] = tail.astype(bf16)


def read_log(message, k, h):
    rows = message.shape[2] - EXTRA
    tail = message[k, h, rows:].astype(f32)
    return tail[0:1] + tail[1:2] + tail[2:3]


def upstream_kernel(
    grad, panel, gate, saved, cumulative, out_group, gate_grad, scan_grad, message, total
):
    step = pl.program_id(0)
    quarters, blocks, rows, columns = panel.shape
    weights = jnp.concatenate(
        [panel[:, b].reshape(quarters * rows, columns) for b in range(blocks)], axis=1
    )
    product = lax.dot_general(grad[...], weights, NT, preferred_element_type=f32)

    @pl.when(step == 0)
    def _():
        total[...] = product

    @pl.when(step > 0)
    def _():
        total[...] += product

    @pl.when(step == pl.num_programs(0) - 1)
    def _():
        upstream = total[...]
        value = gate[...].astype(f32)
        sig = jax.nn.sigmoid(value)
        gate_grad[...] = (
            upstream * saved[...].astype(f32) * sig * (1.0 + value * (1.0 - sig))
        ).astype(bf16)
        scan = (upstream * (value * sig)).astype(bf16)
        scan_grad[...] = scan
        heads = cumulative.shape[1]
        width = scan.shape[1] // heads
        weighted = scan.astype(f32) * by_head(jnp.exp(cumulative[...]), width)
        local = lax.dot_general(
            weighted.astype(bf16), out_group[...], TN, preferred_element_type=f32
        )
        states = local.shape[1]
        for h in range(heads):
            term = local[h * width : (h + 1) * width].astype(bf16)
            for k in range(message.shape[0]):
                message[k, h, :width] = term
            last = jnp.broadcast_to(cumulative[cumulative.shape[0] - 1 :, h : h + 1], (1, states))
            write_log(message, h, last)


def row_kernel(x_ref, *refs):
    received, (message, in_row, tail_log) = refs[:RING], refs[RING:]
    x = x_ref[0]
    _, heads, rows, states = message.shape
    width = rows - EXTRA
    for h in range(heads):
        carry = jnp.zeros((width, states), f32)
        logs = jnp.zeros((1, states), f32)

        def further(j, keep, carry, logs):
            log = read_log(received[j], 0, h)
            term = received[j][0, h, :width].astype(f32) + jnp.exp(log) * carry
            return jnp.where(keep, term, carry), jnp.where(keep, logs + log, logs)

        for j in reversed(range(1, RING)):
            carry, logs = further(j, x + j < RING, carry, logs)
        in_row[h] = carry
        tail_log[h] = jnp.broadcast_to(logs, tail_log.shape[1:])
        carry, logs = further(0, x >= 0, carry, logs)
        for j in reversed(range(1, RING)):
            carry, logs = further(j, x + j >= RING, carry, logs)
        message[0, h, :width] = carry.astype(bf16)
        write_log(message, h, logs)


def inside_kernel(in_group, out_group, cumulative, turned, scan_grad, step_size, skip_gain, out):
    length, heads = cumulative.shape
    width = scan_grad.shape[1] // heads
    size = 128
    for start in range(0, length, size):
        here = slice(start, start + size)
        dots = lax.dot_general(
            in_group[here], out_group[start:], NT, preferred_element_type=f32
        )
        t = lax.broadcasted_iota(jnp.int32, dots.shape, 0)
        s = lax.broadcasted_iota(jnp.int32, dots.shape, 1)
        terms = []
        for h in range(heads):
            spread = turned[h : h + 1, start:] - cumulative[here, h : h + 1]
            factor = jnp.where(t <= s, jnp.exp(jnp.minimum(spread, 0.0)), 0.0)
            terms.append(
                jnp.dot(
                    (dots * factor).astype(bf16),
                    scan_grad[start:, h * width : (h + 1) * width],
                    preferred_element_type=f32,
                )
            )
        inside = jnp.concatenate(terms, axis=1)
        out[here] = by_head(step_size[here], width) * inside + by_head(
            jnp.broadcast_to(skip_gain[...], (size, heads)), width
        ) * scan_grad[here].astype(f32)


def carried_kernel(rows_z, z_ref, *refs):
    received = refs[: rows_z - 1]
    in_row, tail_log, in_group, cumulative, step_size, partial, out = refs[rows_z - 1 :]
    z = z_ref[0]
    _, heads, rows, states = received[0].shape
    width = rows - EXTRA
    length = cumulative.shape[0]
    terms = []
    for h in range(heads):
        carry = jnp.zeros((width, states), f32)
        for j in reversed(range(1, rows_z)):
            message = received[j - 1]
            term = message[0, h, :width].astype(f32)
            term = term + jnp.exp(read_log(message, 0, h)) * carry
            carry = jnp.where(z + j < rows_z, term, carry)
        carried = in_row[h] + jnp.exp(tail_log[h, 0:1]) * carry
        terms.append(
            lax.dot_general(in_group[...], carried.astype(bf16), NT, preferred_element_type=f32)
        )
    decay = jnp.exp(cumulative[length - 1 :] - cumulative[...])
    scale = by_head(step_size[...] * decay, width)
    out[...] = (partial[...] + scale * jnp.concatenate(terms, axis=1)).astype(bf16)


def cost(flops, bytes_accessed, transcendentals=0):
    return pl.CostEstimate(
        flops=flops, bytes_accessed=bytes_accessed, transcendentals=transcendentals
    )


def along_x(block, step):
    rows = lax.axis_size("seq")
    route = [(i, i // RING * RING + (i + step) % RING) for i in range(rows)]
    return lax.ppermute(block, "seq", route)


def along_z(block, step):
    size = lax.axis_size("seq")
    return lax.ppermute(block, "seq", [(i, (i + RING * step) % size) for i in range(size)])


def total_of(*terms):
    return sum(t.astype(f32) for t in terms).astype(bf16)


def to_group(blocks, groups):
    return lax.all_to_all(
        blocks, "seq", split_axis=0, concat_axis=0, tiled=True, axis_index_groups=groups
    )


def after(value, *others):
    return lax.optimization_barrier((value, *others))[0]


def on_device(
    out_grad,
    out_weight,
    gate_input,
    scan_output,
    step_size,
    log_decay,
    input_map,
    output_map,
    skip_gain,
):
    length, width = out_grad.shape
    heads_here = log_decay.shape[1]
    columns_here = gate_input.shape[1]
    head_width = columns_here // heads_here
    seq_size = lax.axis_size("seq")
    head_size = lax.axis_size("head")
    rows_z = seq_size // RING
    quarter = columns_here // RING
    column_block = width // head_size
    states = input_map.shape[2]
    message_rows = head_width + EXTRA
    me = lax.axis_index("seq")
    x = (me % RING).astype(jnp.int32)
    z = (me // RING).astype(jnp.int32)
    rings = [[r * RING + i for i in range(RING)] for r in range(rows_z)]
    steps = 2
    blocks = head_size // steps
    wide = blocks * column_block

    half = head_size // 2
    whole = lambda shape: pl.BlockSpec(shape, lambda *_: (0,) * len(shape))
    block_shape = (half, quarter, column_block)
    quarter_shape = (head_size, quarter, column_block)
    x_place = x.reshape(1)
    own, forth, opposite, back = pl.pallas_call(
        functools.partial(part_kernel, 1.0 / math.sqrt(length * seq_size)),
        name="block_parts",
        grid=(2,),
        in_specs=[
            SMEM,
            whole((length, columns_here)),
            whole((length, columns_here)),
            pl.BlockSpec((length, half * column_block), lambda i: (0, i)),
        ],
        out_specs=[pl.BlockSpec(block_shape, lambda i: (i, 0, 0))] * RING,
        out_shape=[jax.ShapeDtypeStruct(quarter_shape, bf16)] * RING,
        scratch_shapes=[
            pltpu.VMEM((columns_here, length), f32),
            pltpu.VMEM((columns_here, length), bf16),
        ],
        cost_estimate=cost(2 * length * width * columns_here, 2 * length * width),
    )(x_place, gate_input, scan_output, out_grad)
    window = window_starts(rows_z, half)[0]
    z_place = z.reshape(1)
    windows = pl.pallas_call(
        functools.partial(ring_sum_kernel, rows_z),
        name="ring_sum",
        in_specs=[SMEM] + [VMEM] * RING,
        out_specs=[VMEM] * (2 * rows_z),
        out_shape=[jax.ShapeDtypeStruct((window, quarter, column_block), bf16)] * (2 * rows_z),
        cost_estimate=cost(10**6, 4 * 10**6),
    )(z_place, own, along_x(opposite, 2), along_x(forth, 1), along_x(back, -1))
    windows_a, windows_b = windows[:rows_z], windows[rows_z:]
    reduced = [
        total_of(w[0], *(along_z(w[j], j) for j in range(1, rows_z)))
        for w in (windows_a, windows_b)
    ]
    gathered = [r if j == 0 else along_z(r, -j) for r in reduced for j in range(rows_z)]

    group_index = lax.axis_index("head") * heads_here // (HEAD_COUNT // G)
    in_group = lax.dynamic_index_in_dim(input_map, group_index, 1, keepdims=False)
    out_group = lax.dynamic_index_in_dim(output_map, group_index, 1, keepdims=False)
    cumulative = jnp.cumsum(log_decay, axis=0)
    turned = cumulative.T

    weight_quarter = lax.dynamic_index_in_dim(
        out_weight.reshape(head_size, RING, quarter, column_block),
        x,
        1,
        keepdims=False,
    )
    rows_quarter = lax.all_to_all(weight_quarter, "head", split_axis=0, concat_axis=0, tiled=True)
    rows_quarter, in_group, out_group, cumulative, turned, step_size, _, _ = lax.optimization_barrier(
        (
            rows_quarter,
            in_group,
            out_group,
            cumulative,
            turned,
            step_size,
            windows_a[0],
            windows_b[0],
        )
    )
    panel = to_group(jnp.broadcast_to(rows_quarter[None], (RING, *rows_quarter.shape)), rings)
    panel = after(panel, *reduced)

    panel_shape = (length, columns_here)
    gate_grad, scan_grad, message = pl.pallas_call(
        upstream_kernel,
        name="upstream",
        grid=(steps,),
        in_specs=[
            pl.BlockSpec((length, wide), lambda i: (0, i)),
            pl.BlockSpec((RING, blocks, quarter, column_block), lambda i: (0, i, 0, 0)),
            whole(panel_shape),
            whole(panel_shape),
            whole((length, heads_here)),
            whole((length, states)),
        ],
        out_specs=[
            whole(panel_shape),
            whole(panel_shape),
            whole((1, heads_here, message_rows, states)),
        ],
        out_shape=[
            jax.ShapeDtypeStruct(panel_shape, bf16),
            jax.ShapeDtypeStruct(panel_shape, bf16),
            jax.ShapeDtypeStruct((1, heads_here, message_rows, states), bf16),
        ],
        scratch_shapes=[pltpu.VMEM(panel_shape, f32)],
        cost_estimate=cost(2 * length * width * columns_here, 2 * length * width),
    )(out_grad, panel, gate_input, scan_output, cumulative, out_group)

    state = (heads_here, head_width, states)
    on_ring = [message if j == 0 else along_x(message, -j) for j in range(RING)]
    quarter_sum = pl.pallas_call(
        functools.partial(assemble_kernel, rows_z),
        name="assemble",
        in_specs=[SMEM] + [VMEM] * (2 * rows_z),
        out_specs=VMEM,
        out_shape=jax.ShapeDtypeStruct((head_size, quarter, column_block), bf16),
        cost_estimate=cost(10**5, 10**6),
    )(z_place, *gathered)
    pieces = lax.all_to_all(quarter_sum, "head", split_axis=0, concat_axis=0, tiled=True)
    pieces = after(pieces, *on_ring)
    quarters = [pieces, along_x(pieces, -1), along_x(pieces, 2), along_x(pieces, 1)]
    weight_grad = jnp.zeros((head_size, RING, quarter, column_block), bf16)
    for j in (0, 2, 1, 3):
        weight_grad = lax.dynamic_update_slice_in_dim(
            weight_grad, quarters[j][:, None], (x + j) % RING, 1
        )
    weight_grad = weight_grad.reshape(head_size * columns_here, column_block)

    partial = pl.pallas_call(
        inside_kernel,
        name="inside",
        in_specs=[VMEM] * 7,
        out_specs=VMEM,
        out_shape=jax.ShapeDtypeStruct(panel_shape, f32),
        cost_estimate=cost(10**3, 10**3),
    )(
        in_group,
        out_group,
        cumulative,
        turned,
        after(scan_grad, pieces),
        step_size,
        skip_gain.reshape(1, heads_here),
    )
    row_message, in_row, tail_log = pl.pallas_call(
        row_kernel,
        name="row_scan",
        in_specs=[SMEM] + [VMEM] * RING,
        out_specs=[VMEM, VMEM, VMEM],
        out_shape=[
            jax.ShapeDtypeStruct((1, heads_here, message_rows, states), bf16),
            jax.ShapeDtypeStruct(state, f32),
            jax.ShapeDtypeStruct((heads_here, 8, states), f32),
        ],
        cost_estimate=cost(10**3, 10**3),
    )(x_place, *on_ring)
    from_rows = [
        lax.ppermute(
            row_message, "seq", [(i + j * RING, i) for i in range(seq_size - j * RING)]
        )
        for j in range(1, rows_z)
    ]
    input_grad = pl.pallas_call(
        functools.partial(carried_kernel, rows_z),
        name="carried",
        in_specs=[SMEM] + [VMEM] * (5 + rows_z),
        out_specs=VMEM,
        out_shape=jax.ShapeDtypeStruct(panel_shape, bf16),
        cost_estimate=cost(10**3, 10**3),
    )(z.reshape(1), *from_rows, in_row, tail_log, in_group, cumulative, step_size, partial)

    return (input_grad, gate_grad, weight_grad)


def solution(mesh):
    in_specs = (
        P("seq", None),
        P(None, "head"),
        P("seq", "head"),
        P("seq", "head"),
        P("seq", "head"),
        P("seq", "head"),
        P("seq", None, None),
        P("seq", None, None),
        P("head"),
    )
    out_specs = (P("seq", "head"), P("seq", "head"), P(None, "head"))
    return jax.shard_map(
        on_device, mesh=mesh, in_specs=in_specs, out_specs=out_specs, check_vma=False
    )
```

```python
import functools
import math

import jax
import jax.numpy as jnp
from jax import lax
from jax.experimental import pallas as pl
from jax.experimental.pallas import tpu as pltpu
from jax.sharding import PartitionSpec as P

HEAD_COUNT = 128
G = 4
RING = 4
EXTRA = 16
ORDER_STEPS = 4

f32 = jnp.float32
bf16 = jnp.bfloat16
VMEM = pl.BlockSpec(memory_space=pltpu.VMEM)
SMEM = pl.BlockSpec(memory_space=pltpu.SMEM)
NT = (((1,), (1,)), ((), ()))
TN = (((0,), (0,)), ((), ()))


def by_head(columns, width):
    rows, heads = columns.shape
    head = lax.broadcasted_iota(jnp.int32, (rows, heads * width), 1) // width
    out = jnp.broadcast_to(columns[:, :1], (rows, heads * width))
    for h in range(1, heads):
        out = jnp.where(head == h, columns[:, h : h + 1], out)
    return out


def part_kernel(scale, x_ref, gate, saved, grad, *rest):
    outs, turned, ordered = rest[:RING], rest[RING], rest[RING + 1]
    blocks, rows, columns = outs[0].shape

    @pl.when(pl.program_id(0) == 0)
    def _():
        value = gate[...].astype(f32)
        gated = saved[...].astype(f32) * (value * jax.nn.sigmoid(value))
        turned[...] = gated.T
        for j in range(RING):
            start = pl.multiple_of((x_ref[0] + j) % RING * rows, rows)
            ordered[j * rows : (j + 1) * rows] = turned[pl.ds(start, rows)].astype(bf16)

    product = jnp.dot(ordered[...], grad[...], preferred_element_type=f32) * scale
    for b in range(blocks):
        piece = product[:, b * columns : (b + 1) * columns].astype(bf16)
        for j in range(RING):
            outs[j][b] = piece[j * rows : (j + 1) * rows]


def window_starts(rows_z, half):
    window = -(-half // rows_z)
    return window, [k * (half - window) // (rows_z - 1) for k in range(rows_z)]


def window_of(rows_z, half, k):
    starts = window_starts(rows_z, half)[1]
    k = k % rows_z
    start = jnp.int32(starts[0])
    for i in range(1, rows_z):
        start = jnp.where(k == i, starts[i], start)
    return start


def ring_sum_kernel(rows_z, z_ref, *refs):
    terms, outs = refs[:RING], refs[RING:]
    half, window = terms[0].shape[0] // 2, outs[0].shape[0]
    for which in range(2):
        for j in range(rows_z):
            rows = pl.ds(window_of(rows_z, half, z_ref[0] + j) + which * half, window)
            outs[which * rows_z + j][...] = sum(t[rows].astype(f32) for t in terms).astype(bf16)


def assemble_kernel(rows_z, z_ref, *refs):
    pieces, out = refs[:-1], refs[-1]
    half = out.shape[0] // 2
    window = pieces[0].shape[0]
    for which in range(2):
        for j in range(rows_z):
            start = window_of(rows_z, half, z_ref[0] + j) + which * half
            out[pl.ds(start, window)] = pieces[which * rows_z + j][...]


def order_kernel(x_ref, *refs):
    quarters, out = refs[:RING], refs[RING]
    for j in range(RING):
        out[:, pl.ds((x_ref[0] + j) % RING, 1)] = quarters[j][...][:, None]


def write_log(message, h, total):
    rows = message.shape[2] - EXTRA
    high = total.astype(bf16).astype(f32)
    middle = (total - high).astype(bf16).astype(f32)
    low = total - high - middle
    place = lax.broadcasted_iota(jnp.int32, (EXTRA, total.shape[1]), 0)
    tail = jnp.where(
        place == 0, high, jnp.where(place == 1, middle, jnp.where(place == 2, low, 0.0))
    )
    for k in range(message.shape[0]):
        message[k, h, rows:] = tail.astype(bf16)


def read_log(message, k, h):
    rows = message.shape[2] - EXTRA
    tail = message[k, h, rows:].astype(f32)
    return tail[0:1] + tail[1:2] + tail[2:3]


def upstream_kernel(
    grad, panel, gate, saved, cumulative, out_group, gate_grad, scan_grad, message, total
):
    step = pl.program_id(0)
    quarters, blocks, rows, columns = panel.shape
    weights = jnp.concatenate(
        [panel[:, b].reshape(quarters * rows, columns) for b in range(blocks)], axis=1
    )
    product = lax.dot_general(grad[...], weights, NT, preferred_element_type=f32)

    @pl.when(step == 0)
    def _():
        total[...] = product

    @pl.when(step > 0)
    def _():
        total[...] += product

    @pl.when(step == pl.num_programs(0) - 1)
    def _():
        upstream = total[...]
        value = gate[...].astype(f32)
        sig = jax.nn.sigmoid(value)
        gate_grad[...] = (
            upstream * saved[...].astype(f32) * sig * (1.0 + value * (1.0 - sig))
        ).astype(bf16)
        scan = (upstream * (value * sig)).astype(bf16)
        scan_grad[...] = scan
        heads = cumulative.shape[1]
        width = scan.shape[1] // heads
        weighted = scan.astype(f32) * by_head(jnp.exp(cumulative[...]), width)
        local = lax.dot_general(
            weighted.astype(bf16), out_group[...], TN, preferred_element_type=f32
        )
        states = local.shape[1]
        for h in range(heads):
            term = local[h * width : (h + 1) * width].astype(bf16)
            for k in range(message.shape[0]):
                message[k, h, :width] = term
            last = jnp.broadcast_to(cumulative[cumulative.shape[0] - 1 :, h : h + 1], (1, states))
            write_log(message, h, last)


def row_kernel(x_ref, *refs):
    received, (message, in_row, tail_log) = refs[:RING], refs[RING:]
    x = x_ref[0]
    _, heads, rows, states = message.shape
    width = rows - EXTRA
    for h in range(heads):
        carry = jnp.zeros((width, states), f32)
        logs = jnp.zeros((1, states), f32)

        def further(j, keep, carry, logs):
            log = read_log(received[j], 0, h)
            term = received[j][0, h, :width].astype(f32) + jnp.exp(log) * carry
            return jnp.where(keep, term, carry), jnp.where(keep, logs + log, logs)

        for j in reversed(range(1, RING)):
            carry, logs = further(j, x + j < RING, carry, logs)
        in_row[h] = carry
        tail_log[h] = jnp.broadcast_to(logs, tail_log.shape[1:])
        carry, logs = further(0, x >= 0, carry, logs)
        for j in reversed(range(1, RING)):
            carry, logs = further(j, x + j >= RING, carry, logs)
        message[0, h, :width] = carry.astype(bf16)
        write_log(message, h, logs)


def inside_kernel(in_group, out_group, cumulative, turned, scan_grad, step_size, skip_gain, out):
    length, heads = cumulative.shape
    width = scan_grad.shape[1] // heads
    size = 128
    for start in range(0, length, size):
        here = slice(start, start + size)
        dots = lax.dot_general(
            in_group[here], out_group[start:], NT, preferred_element_type=f32
        )
        t = lax.broadcasted_iota(jnp.int32, dots.shape, 0)
        s = lax.broadcasted_iota(jnp.int32, dots.shape, 1)
        terms = []
        for h in range(heads):
            spread = turned[h : h + 1, start:] - cumulative[here, h : h + 1]
            factor = jnp.where(t <= s, jnp.exp(jnp.minimum(spread, 0.0)), 0.0)
            terms.append(
                jnp.dot(
                    (dots * factor).astype(bf16),
                    scan_grad[start:, h * width : (h + 1) * width],
                    preferred_element_type=f32,
                )
            )
        inside = jnp.concatenate(terms, axis=1)
        out[here] = by_head(step_size[here], width) * inside + by_head(
            jnp.broadcast_to(skip_gain[...], (size, heads)), width
        ) * scan_grad[here].astype(f32)


def carried_kernel(rows_z, z_ref, *refs):
    received = refs[: rows_z - 1]
    in_row, tail_log, in_group, cumulative, step_size, partial, out = refs[rows_z - 1 :]
    z = z_ref[0]
    _, heads, rows, states = received[0].shape
    width = rows - EXTRA
    length = cumulative.shape[0]
    terms = []
    for h in range(heads):
        carry = jnp.zeros((width, states), f32)
        for j in reversed(range(1, rows_z)):
            message = received[j - 1]
            term = message[0, h, :width].astype(f32)
            term = term + jnp.exp(read_log(message, 0, h)) * carry
            carry = jnp.where(z + j < rows_z, term, carry)
        carried = in_row[h] + jnp.exp(tail_log[h, 0:1]) * carry
        terms.append(
            lax.dot_general(in_group[...], carried.astype(bf16), NT, preferred_element_type=f32)
        )
    decay = jnp.exp(cumulative[length - 1 :] - cumulative[...])
    scale = by_head(step_size[...] * decay, width)
    out[...] = (partial[...] + scale * jnp.concatenate(terms, axis=1)).astype(bf16)


def cost(flops, bytes_accessed, transcendentals=0):
    return pl.CostEstimate(
        flops=flops, bytes_accessed=bytes_accessed, transcendentals=transcendentals
    )


def along_x(block, step):
    rows = lax.axis_size("seq")
    route = [(i, i // RING * RING + (i + step) % RING) for i in range(rows)]
    return lax.ppermute(block, "seq", route)


def along_z(block, step):
    size = lax.axis_size("seq")
    return lax.ppermute(block, "seq", [(i, (i + RING * step) % size) for i in range(size)])


def total_of(*terms):
    return sum(t.astype(f32) for t in terms).astype(bf16)


def to_group(blocks, groups):
    return lax.all_to_all(
        blocks, "seq", split_axis=0, concat_axis=0, tiled=True, axis_index_groups=groups
    )


def after(value, *others):
    return lax.optimization_barrier((value, *others))[0]


def on_device(
    out_grad,
    out_weight,
    gate_input,
    scan_output,
    step_size,
    log_decay,
    input_map,
    output_map,
    skip_gain,
):
    length, width = out_grad.shape
    heads_here = log_decay.shape[1]
    columns_here = gate_input.shape[1]
    head_width = columns_here // heads_here
    seq_size = lax.axis_size("seq")
    head_size = lax.axis_size("head")
    rows_z = seq_size // RING
    quarter = columns_here // RING
    column_block = width // head_size
    states = input_map.shape[2]
    message_rows = head_width + EXTRA
    me = lax.axis_index("seq")
    x = (me % RING).astype(jnp.int32)
    z = (me // RING).astype(jnp.int32)
    rings = [[r * RING + i for i in range(RING)] for r in range(rows_z)]
    steps = 2
    blocks = head_size // steps
    wide = blocks * column_block

    half = head_size // 2
    whole = lambda shape: pl.BlockSpec(shape, lambda *_: (0,) * len(shape))
    block_shape = (half, quarter, column_block)
    quarter_shape = (head_size, quarter, column_block)
    x_place = x.reshape(1)
    own, forth, opposite, back = pl.pallas_call(
        functools.partial(part_kernel, 1.0 / math.sqrt(length * seq_size)),
        name="block_parts",
        grid=(2,),
        in_specs=[
            SMEM,
            whole((length, columns_here)),
            whole((length, columns_here)),
            pl.BlockSpec((length, half * column_block), lambda i: (0, i)),
        ],
        out_specs=[pl.BlockSpec(block_shape, lambda i: (i, 0, 0))] * RING,
        out_shape=[jax.ShapeDtypeStruct(quarter_shape, bf16)] * RING,
        scratch_shapes=[
            pltpu.VMEM((columns_here, length), f32),
            pltpu.VMEM((columns_here, length), bf16),
        ],
        cost_estimate=cost(2 * length * width * columns_here, 2 * length * width),
    )(x_place, gate_input, scan_output, out_grad)
    window = window_starts(rows_z, half)[0]
    z_place = z.reshape(1)
    windows = pl.pallas_call(
        functools.partial(ring_sum_kernel, rows_z),
        name="ring_sum",
        in_specs=[SMEM] + [VMEM] * RING,
        out_specs=[VMEM] * (2 * rows_z),
        out_shape=[jax.ShapeDtypeStruct((window, quarter, column_block), bf16)] * (2 * rows_z),
        cost_estimate=cost(10**6, 4 * 10**6),
    )(z_place, own, along_x(opposite, 2), along_x(forth, 1), along_x(back, -1))
    windows_a, windows_b = windows[:rows_z], windows[rows_z:]
    reduced = [
        total_of(w[0], *(along_z(w[j], j) for j in range(1, rows_z)))
        for w in (windows_a, windows_b)
    ]
    gathered = [r if j == 0 else along_z(r, -j) for r in reduced for j in range(rows_z)]

    group_index = lax.axis_index("head") * heads_here // (HEAD_COUNT // G)
    in_group = lax.dynamic_index_in_dim(input_map, group_index, 1, keepdims=False)
    out_group = lax.dynamic_index_in_dim(output_map, group_index, 1, keepdims=False)
    cumulative = jnp.cumsum(log_decay, axis=0)
    turned = cumulative.T

    weight_quarter = lax.dynamic_index_in_dim(
        out_weight.reshape(head_size, RING, quarter, column_block),
        x,
        1,
        keepdims=False,
    )
    rows_quarter = lax.all_to_all(weight_quarter, "head", split_axis=0, concat_axis=0, tiled=True)
    rows_quarter, in_group, out_group, cumulative, turned, step_size, _, _ = lax.optimization_barrier(
        (
            rows_quarter,
            in_group,
            out_group,
            cumulative,
            turned,
            step_size,
            windows_a[0],
            windows_b[0],
        )
    )
    panel = to_group(jnp.broadcast_to(rows_quarter[None], (RING, *rows_quarter.shape)), rings)
    panel = after(panel, *reduced)

    panel_shape = (length, columns_here)
    gate_grad, scan_grad, message = pl.pallas_call(
        upstream_kernel,
        name="upstream",
        grid=(steps,),
        in_specs=[
            pl.BlockSpec((length, wide), lambda i: (0, i)),
            pl.BlockSpec((RING, blocks, quarter, column_block), lambda i: (0, i, 0, 0)),
            whole(panel_shape),
            whole(panel_shape),
            whole((length, heads_here)),
            whole((length, states)),
        ],
        out_specs=[
            whole(panel_shape),
            whole(panel_shape),
            whole((1, heads_here, message_rows, states)),
        ],
        out_shape=[
            jax.ShapeDtypeStruct(panel_shape, bf16),
            jax.ShapeDtypeStruct(panel_shape, bf16),
            jax.ShapeDtypeStruct((1, heads_here, message_rows, states), bf16),
        ],
        scratch_shapes=[pltpu.VMEM(panel_shape, f32)],
        cost_estimate=cost(2 * length * width * columns_here, 2 * length * width),
    )(out_grad, panel, gate_input, scan_output, cumulative, out_group)

    state = (heads_here, head_width, states)
    partial = pl.pallas_call(
        inside_kernel,
        name="inside",
        in_specs=[VMEM] * 7,
        out_specs=VMEM,
        out_shape=jax.ShapeDtypeStruct(panel_shape, f32),
        cost_estimate=cost(10**3, 10**3),
    )(
        in_group,
        out_group,
        cumulative,
        turned,
        scan_grad,
        step_size,
        skip_gain.reshape(1, heads_here),
    )
    on_ring = [message if j == 0 else along_x(message, -j) for j in range(RING)]
    quarter_sum = pl.pallas_call(
        functools.partial(assemble_kernel, rows_z),
        name="assemble",
        in_specs=[SMEM] + [VMEM] * (2 * rows_z),
        out_specs=VMEM,
        out_shape=jax.ShapeDtypeStruct((head_size, quarter, column_block), bf16),
        cost_estimate=cost(10**5, 10**6),
    )(z_place, *gathered)
    pieces = lax.all_to_all(quarter_sum, "head", split_axis=0, concat_axis=0, tiled=True)
    pieces = after(pieces, partial, *on_ring)
    quarters = [pieces, along_x(pieces, -1), along_x(pieces, 2), along_x(pieces, 1)]
    chunk = max(head_size // ORDER_STEPS, 1)
    weight_grad = pl.pallas_call(
        order_kernel,
        name="order",
        grid=(head_size // chunk,),
        in_specs=[SMEM]
        + [pl.BlockSpec((chunk, quarter, column_block), lambda i: (i, 0, 0))] * RING,
        out_specs=pl.BlockSpec((chunk, RING, quarter, column_block), lambda i: (i, 0, 0, 0)),
        out_shape=jax.ShapeDtypeStruct((head_size, RING, quarter, column_block), bf16),
        cost_estimate=cost(10**5, 4 * 10**6),
    )(x_place, *quarters).reshape(head_size * columns_here, column_block)

    row_message, in_row, tail_log = pl.pallas_call(
        row_kernel,
        name="row_scan",
        in_specs=[SMEM] + [VMEM] * RING,
        out_specs=[VMEM, VMEM, VMEM],
        out_shape=[
            jax.ShapeDtypeStruct((1, heads_here, message_rows, states), bf16),
            jax.ShapeDtypeStruct(state, f32),
            jax.ShapeDtypeStruct((heads_here, 8, states), f32),
        ],
        cost_estimate=cost(10**3, 10**3),
    )(x_place, *on_ring)
    from_rows = [
        lax.ppermute(
            row_message, "seq", [(i + j * RING, i) for i in range(seq_size - j * RING)]
        )
        for j in range(1, rows_z)
    ]
    input_grad = pl.pallas_call(
        functools.partial(carried_kernel, rows_z),
        name="carried",
        in_specs=[SMEM] + [VMEM] * (5 + rows_z),
        out_specs=VMEM,
        out_shape=jax.ShapeDtypeStruct(panel_shape, bf16),
        cost_estimate=cost(10**3, 10**3),
    )(z.reshape(1), *from_rows, in_row, tail_log, in_group, cumulative, step_size, partial)

    return (input_grad, gate_grad, weight_grad)


def solution(mesh):
    in_specs = (
        P("seq", None),
        P(None, "head"),
        P("seq", "head"),
        P("seq", "head"),
        P("seq", "head"),
        P("seq", "head"),
        P("seq", None, None),
        P("seq", None, None),
        P("head"),
    )
    out_specs = (P("seq", "head"), P("seq", "head"), P(None, "head"))
    return jax.shard_map(
        on_device, mesh=mesh, in_specs=in_specs, out_specs=out_specs, check_vma=False
    )
```

```python
import functools
import math

import jax
import jax.numpy as jnp
from jax import lax
from jax.experimental import pallas as pl
from jax.experimental.pallas import tpu as pltpu
from jax.sharding import PartitionSpec as P

HEAD_COUNT = 128
G = 4
RING = 4
EXTRA = 16
ORDER_STEPS = 2

f32 = jnp.float32
bf16 = jnp.bfloat16
VMEM = pl.BlockSpec(memory_space=pltpu.VMEM)
SMEM = pl.BlockSpec(memory_space=pltpu.SMEM)
NT = (((1,), (1,)), ((), ()))
TN = (((0,), (0,)), ((), ()))


def by_head(columns, width):
    rows, heads = columns.shape
    head = lax.broadcasted_iota(jnp.int32, (rows, heads * width), 1) // width
    out = jnp.broadcast_to(columns[:, :1], (rows, heads * width))
    for h in range(1, heads):
        out = jnp.where(head == h, columns[:, h : h + 1], out)
    return out


def part_kernel(scale, x_ref, gate, saved, grad, *rest):
    outs, turned, ordered = rest[:RING], rest[RING], rest[RING + 1]
    blocks, rows, columns = outs[0].shape

    @pl.when(pl.program_id(0) == 0)
    def _():
        value = gate[...].astype(f32)
        gated = saved[...].astype(f32) * (value * jax.nn.sigmoid(value))
        turned[...] = gated.T
        for j in range(RING):
            start = pl.multiple_of((x_ref[0] + j) % RING * rows, rows)
            ordered[j * rows : (j + 1) * rows] = turned[pl.ds(start, rows)].astype(bf16)

    product = jnp.dot(ordered[...], grad[...], preferred_element_type=f32) * scale
    for b in range(blocks):
        piece = product[:, b * columns : (b + 1) * columns].astype(bf16)
        for j in range(RING):
            outs[j][b] = piece[j * rows : (j + 1) * rows]


def window_starts(rows_z, half):
    window = -(-half // rows_z)
    return window, [k * (half - window) // (rows_z - 1) for k in range(rows_z)]


def window_of(rows_z, half, k):
    starts = window_starts(rows_z, half)[1]
    k = k % rows_z
    start = jnp.int32(starts[0])
    for i in range(1, rows_z):
        start = jnp.where(k == i, starts[i], start)
    return start


def ring_sum_kernel(rows_z, z_ref, *refs):
    terms, outs = refs[:RING], refs[RING:]
    half, window = terms[0].shape[0] // 2, outs[0].shape[0]
    for which in range(2):
        for j in range(rows_z):
            rows = pl.ds(window_of(rows_z, half, z_ref[0] + j) + which * half, window)
            outs[which * rows_z + j][...] = sum(t[rows].astype(f32) for t in terms).astype(bf16)


def assemble_kernel(rows_z, z_ref, *refs):
    pieces, out = refs[:-1], refs[-1]
    half = out.shape[0] // 2
    window = pieces[0].shape[0]
    for which in range(2):
        for j in range(rows_z):
            start = window_of(rows_z, half, z_ref[0] + j) + which * half
            out[pl.ds(start, window)] = pieces[which * rows_z + j][...]


def order_kernel(x_ref, *refs):
    quarters, out = refs[:-1], refs[-1]
    for j, piece in enumerate(quarters):
        out[:, pl.ds((x_ref[0] + j) % RING, 1)] = piece[...][:, None]


def last_kernel(x_ref, piece, whole, out):
    out[...] = piece[...][:, None]


def write_log(message, h, total):
    rows = message.shape[2] - EXTRA
    high = total.astype(bf16).astype(f32)
    middle = (total - high).astype(bf16).astype(f32)
    low = total - high - middle
    place = lax.broadcasted_iota(jnp.int32, (EXTRA, total.shape[1]), 0)
    tail = jnp.where(
        place == 0, high, jnp.where(place == 1, middle, jnp.where(place == 2, low, 0.0))
    )
    for k in range(message.shape[0]):
        message[k, h, rows:] = tail.astype(bf16)


def read_log(message, k, h):
    rows = message.shape[2] - EXTRA
    tail = message[k, h, rows:].astype(f32)
    return tail[0:1] + tail[1:2] + tail[2:3]


def upstream_kernel(
    grad, panel, gate, saved, cumulative, out_group, gate_grad, scan_grad, message, total
):
    step = pl.program_id(0)
    quarters, blocks, rows, columns = panel.shape
    weights = jnp.concatenate(
        [panel[:, b].reshape(quarters * rows, columns) for b in range(blocks)], axis=1
    )
    product = lax.dot_general(grad[...], weights, NT, preferred_element_type=f32)

    @pl.when(step == 0)
    def _():
        total[...] = product

    @pl.when(step > 0)
    def _():
        total[...] += product

    @pl.when(step == pl.num_programs(0) - 1)
    def _():
        upstream = total[...]
        value = gate[...].astype(f32)
        sig = jax.nn.sigmoid(value)
        gate_grad[...] = (
            upstream * saved[...].astype(f32) * sig * (1.0 + value * (1.0 - sig))
        ).astype(bf16)
        scan = (upstream * (value * sig)).astype(bf16)
        scan_grad[...] = scan
        heads = cumulative.shape[1]
        width = scan.shape[1] // heads
        weighted = scan.astype(f32) * by_head(jnp.exp(cumulative[...]), width)
        local = lax.dot_general(
            weighted.astype(bf16), out_group[...], TN, preferred_element_type=f32
        )
        states = local.shape[1]
        for h in range(heads):
            term = local[h * width : (h + 1) * width].astype(bf16)
            for k in range(message.shape[0]):
                message[k, h, :width] = term
            last = jnp.broadcast_to(cumulative[cumulative.shape[0] - 1 :, h : h + 1], (1, states))
            write_log(message, h, last)


def row_kernel(x_ref, *refs):
    received, (message, in_row, tail_log) = refs[:RING], refs[RING:]
    x = x_ref[0]
    _, heads, rows, states = message.shape
    width = rows - EXTRA
    for h in range(heads):
        carry = jnp.zeros((width, states), f32)
        logs = jnp.zeros((1, states), f32)

        def further(j, keep, carry, logs):
            log = read_log(received[j], 0, h)
            term = received[j][0, h, :width].astype(f32) + jnp.exp(log) * carry
            return jnp.where(keep, term, carry), jnp.where(keep, logs + log, logs)

        for j in reversed(range(1, RING)):
            carry, logs = further(j, x + j < RING, carry, logs)
        in_row[h] = carry
        tail_log[h] = jnp.broadcast_to(logs, tail_log.shape[1:])
        carry, logs = further(0, x >= 0, carry, logs)
        for j in reversed(range(1, RING)):
            carry, logs = further(j, x + j >= RING, carry, logs)
        message[0, h, :width] = carry.astype(bf16)
        write_log(message, h, logs)


def inside_kernel(in_group, out_group, cumulative, turned, scan_grad, step_size, skip_gain, out):
    length, heads = cumulative.shape
    width = scan_grad.shape[1] // heads
    size = 128
    for start in range(0, length, size):
        here = slice(start, start + size)
        dots = lax.dot_general(
            in_group[here], out_group[start:], NT, preferred_element_type=f32
        )
        t = lax.broadcasted_iota(jnp.int32, dots.shape, 0)
        s = lax.broadcasted_iota(jnp.int32, dots.shape, 1)
        terms = []
        for h in range(heads):
            spread = turned[h : h + 1, start:] - cumulative[here, h : h + 1]
            factor = jnp.where(t <= s, jnp.exp(jnp.minimum(spread, 0.0)), 0.0)
            terms.append(
                jnp.dot(
                    (dots * factor).astype(bf16),
                    scan_grad[start:, h * width : (h + 1) * width],
                    preferred_element_type=f32,
                )
            )
        inside = jnp.concatenate(terms, axis=1)
        out[here] = by_head(step_size[here], width) * inside + by_head(
            jnp.broadcast_to(skip_gain[...], (size, heads)), width
        ) * scan_grad[here].astype(f32)


def carried_kernel(rows_z, z_ref, *refs):
    received = refs[: rows_z - 1]
    in_row, tail_log, in_group, cumulative, step_size, partial, out = refs[rows_z - 1 :]
    z = z_ref[0]
    _, heads, rows, states = received[0].shape
    width = rows - EXTRA
    length = cumulative.shape[0]
    terms = []
    for h in range(heads):
        carry = jnp.zeros((width, states), f32)
        for j in reversed(range(1, rows_z)):
            message = received[j - 1]
            term = message[0, h, :width].astype(f32)
            term = term + jnp.exp(read_log(message, 0, h)) * carry
            carry = jnp.where(z + j < rows_z, term, carry)
        carried = in_row[h] + jnp.exp(tail_log[h, 0:1]) * carry
        terms.append(
            lax.dot_general(in_group[...], carried.astype(bf16), NT, preferred_element_type=f32)
        )
    decay = jnp.exp(cumulative[length - 1 :] - cumulative[...])
    scale = by_head(step_size[...] * decay, width)
    out[...] = (partial[...] + scale * jnp.concatenate(terms, axis=1)).astype(bf16)


def cost(flops, bytes_accessed, transcendentals=0):
    return pl.CostEstimate(
        flops=flops, bytes_accessed=bytes_accessed, transcendentals=transcendentals
    )


def along_x(block, step):
    rows = lax.axis_size("seq")
    route = [(i, i // RING * RING + (i + step) % RING) for i in range(rows)]
    return lax.ppermute(block, "seq", route)


def along_z(block, step):
    size = lax.axis_size("seq")
    return lax.ppermute(block, "seq", [(i, (i + RING * step) % size) for i in range(size)])


def total_of(*terms):
    return sum(t.astype(f32) for t in terms).astype(bf16)


def to_group(blocks, groups):
    return lax.all_to_all(
        blocks, "seq", split_axis=0, concat_axis=0, tiled=True, axis_index_groups=groups
    )


def after(value, *others):
    return lax.optimization_barrier((value, *others))[0]


def on_device(
    out_grad,
    out_weight,
    gate_input,
    scan_output,
    step_size,
    log_decay,
    input_map,
    output_map,
    skip_gain,
):
    length, width = out_grad.shape
    heads_here = log_decay.shape[1]
    columns_here = gate_input.shape[1]
    head_width = columns_here // heads_here
    seq_size = lax.axis_size("seq")
    head_size = lax.axis_size("head")
    rows_z = seq_size // RING
    quarter = columns_here // RING
    column_block = width // head_size
    states = input_map.shape[2]
    message_rows = head_width + EXTRA
    me = lax.axis_index("seq")
    x = (me % RING).astype(jnp.int32)
    z = (me // RING).astype(jnp.int32)
    rings = [[r * RING + i for i in range(RING)] for r in range(rows_z)]
    steps = 2
    blocks = head_size // steps
    wide = blocks * column_block

    half = head_size // 2
    whole = lambda shape: pl.BlockSpec(shape, lambda *_: (0,) * len(shape))
    block_shape = (half, quarter, column_block)
    quarter_shape = (head_size, quarter, column_block)
    x_place = x.reshape(1)
    own, forth, opposite, back = pl.pallas_call(
        functools.partial(part_kernel, 1.0 / math.sqrt(length * seq_size)),
        name="block_parts",
        grid=(2,),
        in_specs=[
            SMEM,
            whole((length, columns_here)),
            whole((length, columns_here)),
            pl.BlockSpec((length, half * column_block), lambda i: (0, i)),
        ],
        out_specs=[pl.BlockSpec(block_shape, lambda i: (i, 0, 0))] * RING,
        out_shape=[jax.ShapeDtypeStruct(quarter_shape, bf16)] * RING,
        scratch_shapes=[
            pltpu.VMEM((columns_here, length), f32),
            pltpu.VMEM((columns_here, length), bf16),
        ],
        cost_estimate=cost(2 * length * width * columns_here, 2 * length * width),
    )(x_place, gate_input, scan_output, out_grad)
    weight_quarter = lax.dynamic_index_in_dim(
        out_weight.reshape(head_size, RING, quarter, column_block),
        x,
        1,
        keepdims=False,
    )
    rows_quarter = lax.all_to_all(weight_quarter, "head", split_axis=0, concat_axis=0, tiled=True)
    rows_quarter = jnp.broadcast_to(rows_quarter[None], (RING, *rows_quarter.shape))
    own, rows_quarter = lax.optimization_barrier((own, rows_quarter))
    window = window_starts(rows_z, half)[0]
    z_place = z.reshape(1)
    windows = pl.pallas_call(
        functools.partial(ring_sum_kernel, rows_z),
        name="ring_sum",
        in_specs=[SMEM] + [VMEM] * RING,
        out_specs=[VMEM] * (2 * rows_z),
        out_shape=[jax.ShapeDtypeStruct((window, quarter, column_block), bf16)] * (2 * rows_z),
        cost_estimate=cost(10**6, 4 * 10**6),
    )(z_place, own, along_x(opposite, 2), along_x(forth, 1), along_x(back, -1))
    windows_a, windows_b = windows[:rows_z], windows[rows_z:]
    reduced = [
        total_of(w[0], *(along_z(w[j], j) for j in range(1, rows_z)))
        for w in (windows_a, windows_b)
    ]
    gathered = [r if j == 0 else along_z(r, -j) for r in reduced for j in range(rows_z)]

    group_index = lax.axis_index("head") * heads_here // (HEAD_COUNT // G)
    in_group = lax.dynamic_index_in_dim(input_map, group_index, 1, keepdims=False)
    out_group = lax.dynamic_index_in_dim(output_map, group_index, 1, keepdims=False)
    cumulative = jnp.cumsum(log_decay, axis=0)
    turned = cumulative.T

    rows_quarter, in_group, out_group, cumulative, turned, step_size, _, _ = lax.optimization_barrier(
        (
            rows_quarter,
            in_group,
            out_group,
            cumulative,
            turned,
            step_size,
            windows_a[0],
            windows_b[0],
        )
    )
    panel = to_group(rows_quarter, rings)
    panel = after(panel, *reduced)

    panel_shape = (length, columns_here)
    gate_grad, scan_grad, message = pl.pallas_call(
        upstream_kernel,
        name="upstream",
        grid=(steps,),
        in_specs=[
            pl.BlockSpec((length, wide), lambda i: (0, i)),
            pl.BlockSpec((RING, blocks, quarter, column_block), lambda i: (0, i, 0, 0)),
            whole(panel_shape),
            whole(panel_shape),
            whole((length, heads_here)),
            whole((length, states)),
        ],
        out_specs=[
            whole(panel_shape),
            whole(panel_shape),
            whole((1, heads_here, message_rows, states)),
        ],
        out_shape=[
            jax.ShapeDtypeStruct(panel_shape, bf16),
            jax.ShapeDtypeStruct(panel_shape, bf16),
            jax.ShapeDtypeStruct((1, heads_here, message_rows, states), bf16),
        ],
        scratch_shapes=[pltpu.VMEM(panel_shape, f32)],
        cost_estimate=cost(2 * length * width * columns_here, 2 * length * width),
    )(out_grad, panel, gate_input, scan_output, cumulative, out_group)

    state = (heads_here, head_width, states)
    partial = pl.pallas_call(
        inside_kernel,
        name="inside",
        in_specs=[VMEM] * 7,
        out_specs=VMEM,
        out_shape=jax.ShapeDtypeStruct(panel_shape, f32),
        cost_estimate=cost(10**3, 10**3),
    )(
        in_group,
        out_group,
        cumulative,
        turned,
        scan_grad,
        step_size,
        skip_gain.reshape(1, heads_here),
    )
    on_ring = [message if j == 0 else along_x(message, -j) for j in range(RING)]
    quarter_sum = pl.pallas_call(
        functools.partial(assemble_kernel, rows_z),
        name="assemble",
        in_specs=[SMEM] + [VMEM] * (2 * rows_z),
        out_specs=VMEM,
        out_shape=jax.ShapeDtypeStruct((head_size, quarter, column_block), bf16),
        cost_estimate=cost(10**5, 10**6),
    )(z_place, *gathered)
    pieces = lax.all_to_all(quarter_sum, "head", split_axis=0, concat_axis=0, tiled=True)
    pieces = after(pieces, partial, *on_ring)
    quarters = [pieces, along_x(pieces, -1), along_x(pieces, 2), along_x(pieces, 1)]
    chunk = max(head_size // ORDER_STEPS, 1)
    block = pl.BlockSpec((chunk, quarter, column_block), lambda i, *_: (i, 0, 0))
    weight_shape = jax.ShapeDtypeStruct((head_size, RING, quarter, column_block), bf16)
    weight_grad = pl.pallas_call(
        order_kernel,
        name="order",
        grid=(head_size // chunk,),
        in_specs=[SMEM] + [block] * (RING - 1),
        out_specs=pl.BlockSpec((chunk, RING, quarter, column_block), lambda i: (i, 0, 0, 0)),
        out_shape=weight_shape,
        cost_estimate=cost(10**3, 10**3),
    )(x_place, *quarters[:-1])
    weight_grad = pl.pallas_call(
        last_kernel,
        name="order_last",
        grid_spec=pltpu.PrefetchScalarGridSpec(
            num_scalar_prefetch=1,
            grid=(head_size // chunk,),
            in_specs=[block, pl.BlockSpec(memory_space=pl.ANY)],
            out_specs=pl.BlockSpec(
                (chunk, 1, quarter, column_block),
                lambda i, x_ref: (i, lax.rem(x_ref[0] + RING - 1, RING), 0, 0),
            ),
        ),
        out_shape=weight_shape,
        input_output_aliases={2: 0},
        cost_estimate=cost(10**3, 10**3),
    )(x_place, quarters[-1], weight_grad)
    weight_grad = weight_grad.reshape(head_size * columns_here, column_block)


    row_message, in_row, tail_log = pl.pallas_call(
        row_kernel,
        name="row_scan",
        in_specs=[SMEM] + [VMEM] * RING,
        out_specs=[VMEM, VMEM, VMEM],
        out_shape=[
            jax.ShapeDtypeStruct((1, heads_here, message_rows, states), bf16),
            jax.ShapeDtypeStruct(state, f32),
            jax.ShapeDtypeStruct((heads_here, 8, states), f32),
        ],
        cost_estimate=cost(10**3, 10**3),
    )(x_place, *on_ring)
    from_rows = [
        lax.ppermute(
            row_message, "seq", [(i + j * RING, i) for i in range(seq_size - j * RING)]
        )
        for j in range(1, rows_z)
    ]
    input_grad = pl.pallas_call(
        functools.partial(carried_kernel, rows_z),
        name="carried",
        in_specs=[SMEM] + [VMEM] * (5 + rows_z),
        out_specs=VMEM,
        out_shape=jax.ShapeDtypeStruct(panel_shape, bf16),
        cost_estimate=cost(10**3, 10**3),
    )(z.reshape(1), *from_rows, in_row, tail_log, in_group, cumulative, step_size, partial)

    return (input_grad, gate_grad, weight_grad)


def solution(mesh):
    in_specs = (
        P("seq", None),
        P(None, "head"),
        P("seq", "head"),
        P("seq", "head"),
        P("seq", "head"),
        P("seq", "head"),
        P("seq", None, None),
        P("seq", None, None),
        P("head"),
    )
    out_specs = (P("seq", "head"), P("seq", "head"), P(None, "head"))
    return jax.shard_map(
        on_device, mesh=mesh, in_specs=in_specs, out_specs=out_specs, check_vma=False
    )
```

```python
import functools
import math

import jax
import jax.numpy as jnp
from jax import lax
from jax.experimental import pallas as pl
from jax.experimental.pallas import tpu as pltpu
from jax.sharding import PartitionSpec as P

HEAD_COUNT = 128
G = 4
RING = 4
EXTRA = 16
NEAR = (0, 1, 3)
FAR = 2
ORDER_STEPS = 2

f32 = jnp.float32
bf16 = jnp.bfloat16
VMEM = pl.BlockSpec(memory_space=pltpu.VMEM)
SMEM = pl.BlockSpec(memory_space=pltpu.SMEM)
NT = (((1,), (1,)), ((), ()))
TN = (((0,), (0,)), ((), ()))


def by_head(columns, width):
    rows, heads = columns.shape
    head = lax.broadcasted_iota(jnp.int32, (rows, heads * width), 1) // width
    out = jnp.broadcast_to(columns[:, :1], (rows, heads * width))
    for h in range(1, heads):
        out = jnp.where(head == h, columns[:, h : h + 1], out)
    return out


def part_kernel(scale, x_ref, gate, saved, grad, *rest):
    outs, turned, ordered = rest[:RING], rest[RING], rest[RING + 1]
    blocks, rows, columns = outs[0].shape

    @pl.when(pl.program_id(0) == 0)
    def _():
        value = gate[...].astype(f32)
        gated = saved[...].astype(f32) * (value * jax.nn.sigmoid(value))
        turned[...] = gated.T
        for j in range(RING):
            start = pl.multiple_of((x_ref[0] + j) % RING * rows, rows)
            ordered[j * rows : (j + 1) * rows] = turned[pl.ds(start, rows)].astype(bf16)

    product = jnp.dot(ordered[...], grad[...], preferred_element_type=f32) * scale
    for b in range(blocks):
        piece = product[:, b * columns : (b + 1) * columns].astype(bf16)
        for j in range(RING):
            outs[j][b] = piece[j * rows : (j + 1) * rows]


def window_starts(rows_z, half):
    window = -(-half // rows_z)
    return window, [k * (half - window) // (rows_z - 1) for k in range(rows_z)]


def window_of(rows_z, half, k):
    starts = window_starts(rows_z, half)[1]
    k = k % rows_z
    start = jnp.int32(starts[0])
    for i in range(1, rows_z):
        start = jnp.where(k == i, starts[i], start)
    return start


def ring_sum_kernel(rows_z, z_ref, *refs):
    terms, outs = refs[:RING], refs[RING:]
    half, window = terms[0].shape[0] // 2, outs[0].shape[0]
    for which in range(2):
        for j in range(rows_z):
            rows = pl.ds(window_of(rows_z, half, z_ref[0] + j) + which * half, window)
            outs[which * rows_z + j][...] = sum(t[rows].astype(f32) for t in terms).astype(bf16)


def assemble_kernel(rows_z, z_ref, *refs):
    pieces, out = refs[:-1], refs[-1]
    half = out.shape[0] // 2
    window = pieces[0].shape[0]
    for which in range(2):
        for j in range(rows_z):
            start = window_of(rows_z, half, z_ref[0] + j) + which * half
            out[pl.ds(start, window)] = pieces[which * rows_z + j][...]


def order_kernel(x_ref, *refs):
    quarters, out = refs[:-1], refs[-1]
    for j, piece in zip(NEAR, quarters):
        out[:, pl.ds((x_ref[0] + j) % RING, 1)] = piece[...][:, None]


def last_kernel(x_ref, piece, whole, out):
    out[...] = piece[...][:, None]


def write_log(message, h, total):
    rows = message.shape[2] - EXTRA
    high = total.astype(bf16).astype(f32)
    middle = (total - high).astype(bf16).astype(f32)
    low = total - high - middle
    place = lax.broadcasted_iota(jnp.int32, (EXTRA, total.shape[1]), 0)
    tail = jnp.where(
        place == 0, high, jnp.where(place == 1, middle, jnp.where(place == 2, low, 0.0))
    )
    for k in range(message.shape[0]):
        message[k, h, rows:] = tail.astype(bf16)


def read_log(message, k, h):
    rows = message.shape[2] - EXTRA
    tail = message[k, h, rows:].astype(f32)
    return tail[0:1] + tail[1:2] + tail[2:3]


def upstream_kernel(
    grad, panel, gate, saved, cumulative, out_group, gate_grad, scan_grad, message, total
):
    step = pl.program_id(0)
    quarters, blocks, rows, columns = panel.shape
    weights = jnp.concatenate(
        [panel[:, b].reshape(quarters * rows, columns) for b in range(blocks)], axis=1
    )
    product = lax.dot_general(grad[...], weights, NT, preferred_element_type=f32)

    @pl.when(step == 0)
    def _():
        total[...] = product

    @pl.when(step > 0)
    def _():
        total[...] += product

    @pl.when(step == pl.num_programs(0) - 1)
    def _():
        upstream = total[...]
        value = gate[...].astype(f32)
        sig = jax.nn.sigmoid(value)
        gate_grad[...] = (
            upstream * saved[...].astype(f32) * sig * (1.0 + value * (1.0 - sig))
        ).astype(bf16)
        scan = (upstream * (value * sig)).astype(bf16)
        scan_grad[...] = scan
        heads = cumulative.shape[1]
        width = scan.shape[1] // heads
        weighted = scan.astype(f32) * by_head(jnp.exp(cumulative[...]), width)
        local = lax.dot_general(
            weighted.astype(bf16), out_group[...], TN, preferred_element_type=f32
        )
        states = local.shape[1]
        for h in range(heads):
            term = local[h * width : (h + 1) * width].astype(bf16)
            for k in range(message.shape[0]):
                message[k, h, :width] = term
            last = jnp.broadcast_to(cumulative[cumulative.shape[0] - 1 :, h : h + 1], (1, states))
            write_log(message, h, last)


def row_kernel(x_ref, *refs):
    received, (message, in_row, tail_log) = refs[:RING], refs[RING:]
    x = x_ref[0]
    _, heads, rows, states = message.shape
    width = rows - EXTRA
    for h in range(heads):
        carry = jnp.zeros((width, states), f32)
        logs = jnp.zeros((1, states), f32)

        def further(j, keep, carry, logs):
            log = read_log(received[j], 0, h)
            term = received[j][0, h, :width].astype(f32) + jnp.exp(log) * carry
            return jnp.where(keep, term, carry), jnp.where(keep, logs + log, logs)

        for j in reversed(range(1, RING)):
            carry, logs = further(j, x + j < RING, carry, logs)
        in_row[h] = carry
        tail_log[h] = jnp.broadcast_to(logs, tail_log.shape[1:])
        carry, logs = further(0, x >= 0, carry, logs)
        for j in reversed(range(1, RING)):
            carry, logs = further(j, x + j >= RING, carry, logs)
        message[0, h, :width] = carry.astype(bf16)
        write_log(message, h, logs)


def inside_kernel(in_group, out_group, cumulative, turned, scan_grad, step_size, skip_gain, out):
    length, heads = cumulative.shape
    width = scan_grad.shape[1] // heads
    size = 128
    for start in range(0, length, size):
        here = slice(start, start + size)
        dots = lax.dot_general(
            in_group[here], out_group[start:], NT, preferred_element_type=f32
        )
        t = lax.broadcasted_iota(jnp.int32, dots.shape, 0)
        s = lax.broadcasted_iota(jnp.int32, dots.shape, 1)
        terms = []
        for h in range(heads):
            spread = turned[h : h + 1, start:] - cumulative[here, h : h + 1]
            factor = jnp.where(t <= s, jnp.exp(jnp.minimum(spread, 0.0)), 0.0)
            terms.append(
                jnp.dot(
                    (dots * factor).astype(bf16),
                    scan_grad[start:, h * width : (h + 1) * width],
                    preferred_element_type=f32,
                )
            )
        inside = jnp.concatenate(terms, axis=1)
        out[here] = by_head(step_size[here], width) * inside + by_head(
            jnp.broadcast_to(skip_gain[...], (size, heads)), width
        ) * scan_grad[here].astype(f32)


def carried_kernel(rows_z, z_ref, *refs):
    received = refs[: rows_z - 1]
    in_row, tail_log, in_group, cumulative, step_size, partial, out = refs[rows_z - 1 :]
    z = z_ref[0]
    _, heads, rows, states = received[0].shape
    width = rows - EXTRA
    length = cumulative.shape[0]
    terms = []
    for h in range(heads):
        carry = jnp.zeros((width, states), f32)
        for j in reversed(range(1, rows_z)):
            message = received[j - 1]
            term = message[0, h, :width].astype(f32)
            term = term + jnp.exp(read_log(message, 0, h)) * carry
            carry = jnp.where(z + j < rows_z, term, carry)
        carried = in_row[h] + jnp.exp(tail_log[h, 0:1]) * carry
        terms.append(
            lax.dot_general(in_group[...], carried.astype(bf16), NT, preferred_element_type=f32)
        )
    decay = jnp.exp(cumulative[length - 1 :] - cumulative[...])
    scale = by_head(step_size[...] * decay, width)
    out[...] = (partial[...] + scale * jnp.concatenate(terms, axis=1)).astype(bf16)


def cost(flops, bytes_accessed, transcendentals=0):
    return pl.CostEstimate(
        flops=flops, bytes_accessed=bytes_accessed, transcendentals=transcendentals
    )


def along_x(block, step):
    rows = lax.axis_size("seq")
    route = [(i, i // RING * RING + (i + step) % RING) for i in range(rows)]
    return lax.ppermute(block, "seq", route)


def along_z(block, step):
    size = lax.axis_size("seq")
    return lax.ppermute(block, "seq", [(i, (i + RING * step) % size) for i in range(size)])


def total_of(*terms):
    return sum(t.astype(f32) for t in terms).astype(bf16)


def to_group(blocks, groups):
    return lax.all_to_all(
        blocks, "seq", split_axis=0, concat_axis=0, tiled=True, axis_index_groups=groups
    )


def after(value, *others):
    return lax.optimization_barrier((value, *others))[0]


def on_device(
    out_grad,
    out_weight,
    gate_input,
    scan_output,
    step_size,
    log_decay,
    input_map,
    output_map,
    skip_gain,
):
    length, width = out_grad.shape
    heads_here = log_decay.shape[1]
    columns_here = gate_input.shape[1]
    head_width = columns_here // heads_here
    seq_size = lax.axis_size("seq")
    head_size = lax.axis_size("head")
    rows_z = seq_size // RING
    quarter = columns_here // RING
    column_block = width // head_size
    states = input_map.shape[2]
    message_rows = head_width + EXTRA
    me = lax.axis_index("seq")
    x = (me % RING).astype(jnp.int32)
    z = (me // RING).astype(jnp.int32)
    rings = [[r * RING + i for i in range(RING)] for r in range(rows_z)]
    steps = 2
    blocks = head_size // steps
    wide = blocks * column_block

    half = head_size // 2
    whole = lambda shape: pl.BlockSpec(shape, lambda *_: (0,) * len(shape))
    block_shape = (half, quarter, column_block)
    quarter_shape = (head_size, quarter, column_block)
    x_place = x.reshape(1)
    own, forth, opposite, back = pl.pallas_call(
        functools.partial(part_kernel, 1.0 / math.sqrt(length * seq_size)),
        name="block_parts",
        grid=(2,),
        in_specs=[
            SMEM,
            whole((length, columns_here)),
            whole((length, columns_here)),
            pl.BlockSpec((length, half * column_block), lambda i: (0, i)),
        ],
        out_specs=[pl.BlockSpec(block_shape, lambda i: (i, 0, 0))] * RING,
        out_shape=[jax.ShapeDtypeStruct(quarter_shape, bf16)] * RING,
        scratch_shapes=[
            pltpu.VMEM((columns_here, length), f32),
            pltpu.VMEM((columns_here, length), bf16),
        ],
        cost_estimate=cost(2 * length * width * columns_here, 2 * length * width),
    )(x_place, gate_input, scan_output, out_grad)
    weight_quarter = lax.dynamic_index_in_dim(
        out_weight.reshape(head_size, RING, quarter, column_block),
        x,
        1,
        keepdims=False,
    )
    rows_quarter = lax.all_to_all(weight_quarter, "head", split_axis=0, concat_axis=0, tiled=True)
    rows_quarter = jnp.broadcast_to(rows_quarter[None], (RING, *rows_quarter.shape))
    own, rows_quarter = lax.optimization_barrier((own, rows_quarter))
    window = window_starts(rows_z, half)[0]
    z_place = z.reshape(1)
    windows = pl.pallas_call(
        functools.partial(ring_sum_kernel, rows_z),
        name="ring_sum",
        in_specs=[SMEM] + [VMEM] * RING,
        out_specs=[VMEM] * (2 * rows_z),
        out_shape=[jax.ShapeDtypeStruct((window, quarter, column_block), bf16)] * (2 * rows_z),
        cost_estimate=cost(10**6, 4 * 10**6),
    )(z_place, own, along_x(opposite, 2), along_x(forth, 1), along_x(back, -1))
    windows_a, windows_b = windows[:rows_z], windows[rows_z:]
    reduced = [
        total_of(w[0], *(along_z(w[j], j) for j in range(1, rows_z)))
        for w in (windows_a, windows_b)
    ]
    gathered = [r if j == 0 else along_z(r, -j) for r in reduced for j in range(rows_z)]

    group_index = lax.axis_index("head") * heads_here // (HEAD_COUNT // G)
    in_group = lax.dynamic_index_in_dim(input_map, group_index, 1, keepdims=False)
    out_group = lax.dynamic_index_in_dim(output_map, group_index, 1, keepdims=False)
    cumulative = jnp.cumsum(log_decay, axis=0)
    turned = cumulative.T

    rows_quarter, in_group, out_group, cumulative, turned, step_size, _, _ = lax.optimization_barrier(
        (
            rows_quarter,
            in_group,
            out_group,
            cumulative,
            turned,
            step_size,
            windows_a[0],
            windows_b[0],
        )
    )
    panel = to_group(rows_quarter, rings)
    panel = after(panel, *reduced)

    panel_shape = (length, columns_here)
    gate_grad, scan_grad, message = pl.pallas_call(
        upstream_kernel,
        name="upstream",
        grid=(steps,),
        in_specs=[
            pl.BlockSpec((length, wide), lambda i: (0, i)),
            pl.BlockSpec((RING, blocks, quarter, column_block), lambda i: (0, i, 0, 0)),
            whole(panel_shape),
            whole(panel_shape),
            whole((length, heads_here)),
            whole((length, states)),
        ],
        out_specs=[
            whole(panel_shape),
            whole(panel_shape),
            whole((1, heads_here, message_rows, states)),
        ],
        out_shape=[
            jax.ShapeDtypeStruct(panel_shape, bf16),
            jax.ShapeDtypeStruct(panel_shape, bf16),
            jax.ShapeDtypeStruct((1, heads_here, message_rows, states), bf16),
        ],
        scratch_shapes=[pltpu.VMEM(panel_shape, f32)],
        cost_estimate=cost(2 * length * width * columns_here, 2 * length * width),
    )(out_grad, panel, gate_input, scan_output, cumulative, out_group)

    state = (heads_here, head_width, states)
    partial = pl.pallas_call(
        inside_kernel,
        name="inside",
        in_specs=[VMEM] * 7,
        out_specs=VMEM,
        out_shape=jax.ShapeDtypeStruct(panel_shape, f32),
        cost_estimate=cost(10**3, 10**3),
    )(
        in_group,
        out_group,
        cumulative,
        turned,
        scan_grad,
        step_size,
        skip_gain.reshape(1, heads_here),
    )
    on_ring = [message if j == 0 else along_x(message, -j) for j in range(RING)]
    quarter_sum = pl.pallas_call(
        functools.partial(assemble_kernel, rows_z),
        name="assemble",
        in_specs=[SMEM] + [VMEM] * (2 * rows_z),
        out_specs=VMEM,
        out_shape=jax.ShapeDtypeStruct((head_size, quarter, column_block), bf16),
        cost_estimate=cost(10**5, 10**6),
    )(z_place, *gathered)
    pieces = lax.all_to_all(quarter_sum, "head", split_axis=0, concat_axis=0, tiled=True)
    pieces = after(pieces, partial, *on_ring)
    quarters = [pieces, along_x(pieces, -1), along_x(pieces, 2), along_x(pieces, 1)]
    chunk = max(head_size // ORDER_STEPS, 1)
    block = pl.BlockSpec((chunk, quarter, column_block), lambda i, *_: (i, 0, 0))
    weight_shape = jax.ShapeDtypeStruct((head_size, RING, quarter, column_block), bf16)
    weight_grad = pl.pallas_call(
        order_kernel,
        name="order",
        grid=(head_size // chunk,),
        in_specs=[SMEM] + [block] * (RING - 1),
        out_specs=pl.BlockSpec((chunk, RING, quarter, column_block), lambda i: (i, 0, 0, 0)),
        out_shape=weight_shape,
        cost_estimate=cost(10**3, 10**3),
    )(x_place, *[quarters[j] for j in NEAR])
    weight_grad = pl.pallas_call(
        last_kernel,
        name="order_last",
        grid_spec=pltpu.PrefetchScalarGridSpec(
            num_scalar_prefetch=1,
            grid=(head_size // chunk,),
            in_specs=[block, pl.BlockSpec(memory_space=pl.ANY)],
            out_specs=pl.BlockSpec(
                (chunk, 1, quarter, column_block),
                lambda i, x_ref: (i, lax.rem(x_ref[0] + FAR, RING), 0, 0),
            ),
        ),
        out_shape=weight_shape,
        input_output_aliases={2: 0},
        cost_estimate=cost(10**3, 10**3),
    )(x_place, quarters[FAR], weight_grad)
    weight_grad = weight_grad.reshape(head_size * columns_here, column_block)


    row_message, in_row, tail_log = pl.pallas_call(
        row_kernel,
        name="row_scan",
        in_specs=[SMEM] + [VMEM] * RING,
        out_specs=[VMEM, VMEM, VMEM],
        out_shape=[
            jax.ShapeDtypeStruct((1, heads_here, message_rows, states), bf16),
            jax.ShapeDtypeStruct(state, f32),
            jax.ShapeDtypeStruct((heads_here, 8, states), f32),
        ],
        cost_estimate=cost(10**3, 10**3),
    )(x_place, *on_ring)
    from_rows = [
        lax.ppermute(
            row_message, "seq", [(i + j * RING, i) for i in range(seq_size - j * RING)]
        )
        for j in range(1, rows_z)
    ]
    input_grad = pl.pallas_call(
        functools.partial(carried_kernel, rows_z),
        name="carried",
        in_specs=[SMEM] + [VMEM] * (5 + rows_z),
        out_specs=VMEM,
        out_shape=jax.ShapeDtypeStruct(panel_shape, bf16),
        cost_estimate=cost(10**3, 10**3),
    )(z.reshape(1), *from_rows, in_row, tail_log, in_group, cumulative, step_size, partial)

    return (input_grad, gate_grad, weight_grad)


def solution(mesh):
    in_specs = (
        P("seq", None),
        P(None, "head"),
        P("seq", "head"),
        P("seq", "head"),
        P("seq", "head"),
        P("seq", "head"),
        P("seq", None, None),
        P("seq", None, None),
        P("head"),
    )
    out_specs = (P("seq", "head"), P("seq", "head"), P(None, "head"))
    return jax.shard_map(
        on_device, mesh=mesh, in_specs=in_specs, out_specs=out_specs, check_vma=False
    )
```
